32 devices in a mesh: dp: 2 (over x), ctx: 16 (over z, y, core).
Axes of the slice: x: 2, y: 2, z: 4, core: 2. Of those that a mesh axis runs over, the one named last changes fastest.
Arguments:
- tokens: bfloat16 [24, 1024, 1024], P('dp', 'ctx'), may hold values from -6 to 6
- piece_ids: int32 [24, 1024], P('dp', 'ctx'), may hold values from 0 to 4, as said below
- cotangent: bfloat16 [24, 1024, 1024], P('dp', 'ctx'), may hold values from -6 to 6
- master: float32 [1536, 16, 1024], P(('dp', 'ctx')), may hold values from -1 to 1
- first_moment: float32 [1536, 16, 1024], P(('dp', 'ctx')), may hold values from -20 to 20
- second_moment: float32 [1536, 16, 1024], P(('dp', 'ctx')), may hold values from 12.288 to 122.88
- owner_slot: int32 [768], replicated, may hold values from 0 to 1535, as said below
- vectors: float32 [13, 1024], replicated, may hold values from -0.9 to 1.45
- vector_first: float32 [13, 1024], replicated, may hold values from -96 to 96
- vector_second: float32 [13, 1024], replicated, may hold values from 1228.8 to 19660.8
Outputs:
- mixed: bfloat16 [24, 1024, 1024], P('dp', 'ctx')
- input_grad: float32 [24, 1024, 1024], P('dp', 'ctx')
- bank_grad: float32 [1536, 16, 1024], P(('dp', 'ctx'))
- bank_new: float32 [1536, 16, 1024], P(('dp', 'ctx'))
- first_new: float32 [1536, 16, 1024], P(('dp', 'ctx'))
- second_new: float32 [1536, 16, 1024], P(('dp', 'ctx'))
- vector_grad: float32 [13, 1024], replicated
- vector_new: float32 [13, 1024], replicated
- rows_first: float32 [13, 1024], replicated
- rows_second: float32 [13, 1024], replicated
- factors: float32 [16], replicated
The draws below stay inside these ranges and needn't reach their ends.
Inputs may be any that keep to these rules, and one draw needn't show every extreme that they name: `owner_slot`: slot s lies on device s // 48 of the joined axes dp+ctx, in mesh order; no two blocks share a slot; on one device all 48 slots hold blocks. `piece_ids`: A nonzero id k + 1 marks the whole aligned 256-token span k of its sequence as one picture piece; 0 marks text. The last span of the first sequence is a piece.
All inputs are finite; a program needn't handle non-finite values.
Results may differ from the reference program's by a relative error of at most 0.012.
The reference program's roundings to bfloat16 on the way count: a program that leaves them out, or rounds other values in their place, can miss the bound.
Values may be sent and summed in bfloat16 or wider, within the bound.
No kernel may reach another device: no remote copies, remote signals or barrier semaphores. Data moves between devices by JAX's collectives and lax.ppermute only.
A program may use at most 640 MiB of HBM per device.

```python
import math
import jax
import jax.numpy as jnp
from jax import lax

D = 1024
HEADS = 16
HEAD_DIM = 64
FF = 4096
ROT = 16
PIECE = 256
BLOCK_ROWS = 16
LEN = 1024
BATCH = 24
TOKENS = 24576
NB = 768
CAP = 48
SLOTS = 1536


def owner_table(key):
    key = jax.random.fold_in(key, 7)
    first_key, second_key, third_key = jax.random.split(key, 3)
    chosen = jax.random.randint(first_key, (), 0, SLOTS // CAP)
    order = jax.random.permutation(second_key, SLOTS)
    ranking = jnp.zeros((SLOTS,), jnp.int32).at[order].set(jnp.arange(SLOTS, dtype=jnp.int32))
    device_of = jnp.arange(SLOTS, dtype=jnp.int32) // CAP
    priority = ranking + jnp.where(device_of == chosen, 0, SLOTS)
    picked = jnp.argsort(priority, stable=True)[:NB]
    return jax.random.permutation(third_key, picked).astype(jnp.int32)


def draw_owner_slot(key, part):
    return owner_table(key)


def draw_master(key, part):
    owner_list = owner_table(key)
    block_of = jnp.full((SLOTS,), -1, jnp.int32).at[owner_list].set(jnp.arange(NB, dtype=jnp.int32))
    matrix_of = jnp.maximum(block_of, 0) // (D // BLOCK_ROWS)
    noise_values = jnp.clip(jax.random.normal(jax.random.fold_in(key, 11), (SLOTS, BLOCK_ROWS, D), jnp.float32), -4.0, 4.0)
    head_scale = jnp.exp(jax.random.uniform(jax.random.fold_in(key, 12), (HEADS,), jnp.float32, math.log(0.6), math.log(1.7)))
    column_scale = jnp.repeat(head_scale, HEAD_DIM)
    base_scale = jnp.where(matrix_of >= 8, FF ** (-0.5), D ** (-0.5))
    base_scale = jnp.where(matrix_of == 3, 8.0 * D ** (-0.5), base_scale)
    full_scale = base_scale[:, None, None] * jnp.where((matrix_of < 2)[:, None, None], column_scale[None, None, :], 1.0)
    return jnp.clip(noise_values * full_scale, -1.0, 1.0).astype(jnp.float32)


def draw_vectors(key, part):
    noise_values = jnp.clip(jax.random.normal(jax.random.fold_in(key, 21), (13, D), jnp.float32), -3.0, 3.0)
    row_index = jnp.arange(13)
    gain_rows = ((row_index == 0) | (row_index == 2))[:, None]
    return jnp.where(gain_rows, 1.0 + 0.15 * noise_values, 0.3 * noise_values).astype(jnp.float32)


def draw_piece_ids(key, part):
    span_count = LEN // PIECE
    flags = jax.random.randint(jax.random.fold_in(key, 31), (BATCH, span_count), 0, 2)
    flags = flags.at[0, span_count - 1].set(1)
    labels = (jnp.arange(span_count, dtype=jnp.int32)[None, :] + 1) * flags
    return jnp.repeat(labels, PIECE, axis=1).astype(jnp.int32)


def level_of(rng, dims, cuts, smallest, largest):
    gain = 1.0
    for position, blocks in cuts:
        draws = jax.random.uniform(jax.random.fold_in(jax.random.fold_in(rng, 6), position), (blocks,), jnp.float32, smallest / len(cuts), largest / len(cuts))
        gain = gain * jnp.repeat(jnp.exp(draws), dims[position] // blocks).reshape((-1,) + (1,) * (len(dims) - 1 - position))
    return gain


def scatter_about(rng, shape, deviation, reach, cuts=(), kind=jnp.bfloat16):
    drawn = jax.random.normal(rng, shape, jnp.float32) * deviation
    if len(cuts) > 0:
        drawn = level_of(rng, shape, cuts, -0.22, 0.18) * drawn
    return jnp.clip(drawn, min=-reach, max=reach).astype(kind)


def setup_inputs(seed: int = 0) -> dict:
    arg_keys = jax.random.split(jax.random.key(seed), 11)
    tokens = scatter_about(arg_keys[0], (BATCH, LEN, D), 1.0, 6.0, ((0, 2), (1, 16)))
    piece_ids = draw_piece_ids(jax.random.fold_in(arg_keys[10], 71), 0)
    cotangent = scatter_about(arg_keys[2], (BATCH, LEN, D), 1.0, 6.0, ((0, 2), (1, 16)))
    master = draw_master(jax.random.fold_in(arg_keys[10], 71), 0)
    first_moment = scatter_about(arg_keys[4], (SLOTS, BLOCK_ROWS, D), (0.02 * TOKENS ** 0.5), 20.0, ((0, 32),), jnp.float32)
    second_moment = jnp.clip(jnp.exp(math.log(122.88) - 2.3025851 * jax.random.uniform(arg_keys[5], (SLOTS, BLOCK_ROWS, D), jnp.float32) ** level_of(arg_keys[5], (SLOTS, BLOCK_ROWS, D), ((0, 32),), -0.2, 0.2)), 12.288, 122.88)
    owner_slot = draw_owner_slot(jax.random.fold_in(arg_keys[10], 71), 0)
    vectors = draw_vectors(jax.random.fold_in(arg_keys[10], 71), 0)
    vector_first = scatter_about(arg_keys[8], (13, D), (0.1 * TOKENS ** 0.5), 96.0, (), jnp.float32)
    vector_second = jnp.clip(jnp.exp(jax.random.uniform(arg_keys[9], (13, D), jnp.float32, math.log(1228.8), math.log(19660.8))), 1228.8, 19660.8)
    return dict(tokens=tokens, piece_ids=piece_ids, cotangent=cotangent, master=master, first_moment=first_moment, second_moment=second_moment, owner_slot=owner_slot, vectors=vectors, vector_first=vector_first, vector_second=vector_second)


HIGHEST = lax.Precision.HIGHEST
norm_epsilon = 1e-05
clip_limit = 4.0
beta_first = 0.9
beta_second = 0.95
learn_rate = 0.05
weight_decay = 0.1
adam_epsilon = 1e-08
adam_step = 10.0

@jax.custom_vjp
def low(v):
    return lax.optimization_barrier(v.astype(jnp.bfloat16)).astype(jnp.float32)

@jax.custom_vjp
def low_back(v):
    return v

def low_keep(v):
    return (low(v), None)

def low_pass(kept, grad):
    return (grad,)

def back_keep(v):
    return (v, None)

def back_low(kept, grad):
    return (low(grad),)
low.defvjp(low_keep, low_pass)
low_back.defvjp(back_keep, back_low)

def layer_norm(values_in, gain_row, bias_row):
    center = values_in - lax.optimization_barrier(jnp.mean(values_in, -1, keepdims=True))
    spread = lax.optimization_barrier(jnp.mean(center * center, -1, keepdims=True))
    return center * lax.rsqrt(spread + norm_epsilon) * gain_row + bias_row

def rotary_tables(positions):
    halves = jnp.arange(ROT // 2, dtype=jnp.float32)
    inverse = jnp.exp(-math.log(10000.0) * 2.0 * halves / ROT)
    angles = positions[:, None] * inverse[None, :]
    angles = jnp.concatenate([angles, angles], -1)
    return (jnp.cos(angles), jnp.sin(angles))

def rotate(heads_in, cosines, sines):
    midpoint = ROT // 2
    leading = heads_in[..., :ROT]
    turned = jnp.concatenate([-leading[..., midpoint:], leading[..., :midpoint]], -1)
    rotated = leading * cosines[:, None, :] + turned * sines[:, None, :]
    return jnp.concatenate([rotated, heads_in[..., ROT:]], -1)

def adamw_update(weight, gradient, moment_one, moment_two, decay_rate):
    moment_one = beta_first * moment_one + (1.0 - beta_first) * gradient
    moment_two = beta_second * moment_two + (1.0 - beta_second) * gradient * gradient
    first_hat = moment_one / (1.0 - beta_first ** adam_step)
    second_hat = moment_two / (1.0 - beta_second ** adam_step)
    weight = weight - learn_rate * (first_hat / (jnp.sqrt(second_hat) + adam_epsilon) + decay_rate * weight)
    return (weight, moment_one, moment_two)

def attend(query_block, query_positions, query_pieces, keys, values, key_positions, key_pieces):
    scores = jnp.einsum('qhd,khd->hqk', query_block, keys, precision=HIGHEST) * HEAD_DIM ** (-0.5)
    scores = low_back(scores)
    visible = (key_positions[None, :] <= query_positions[:, None]) | (query_pieces[:, None] > 0) & (query_pieces[:, None] == key_pieces[None, :])
    scores = jnp.where(visible[None], scores, -1e+30)
    row_top = lax.optimization_barrier(jnp.max(scores, -1, keepdims=True))
    log_total = row_top + jnp.log(lax.optimization_barrier(jnp.sum(jnp.exp(scores - row_top), -1, keepdims=True)))
    weights = jnp.exp(scores - log_total)
    result = jnp.einsum('hqk,khd->qhd', low(weights), values, precision=HIGHEST)
    return (result, lax.optimization_barrier(jnp.max(row_top, axis=(1, 2))))

def reference(tokens, piece_ids, cotangent, master, first_moment, second_moment, owner_slot, vectors, vector_first, vector_second):
    block_index = jnp.arange(NB, dtype=jnp.int32)
    slot_block = jnp.full((SLOTS,), -1, dtype=jnp.int32).at[owner_slot].set(block_index)
    matrices = low(master[owner_slot]).reshape(12, D, D)
    weight_qkv = jnp.concatenate([matrices[0], matrices[1], matrices[2]], 1)
    weight_up = matrices[4:8].transpose(1, 0, 2).reshape(D, FF)
    weight_down = matrices[8:12].reshape(FF, D)
    params = (weight_qkv, matrices[3], weight_up, weight_down, vectors)
    cosines, sines = rotary_tables(jnp.arange(LEN, dtype=jnp.float32))
    positions = jnp.arange(LEN, dtype=jnp.int32)
    block_rows = min(512, LEN)
    block_count = LEN // block_rows

    def one_sequence(params, inputs, pieces):
        weight_qkv, weight_out, weight_up, weight_down, vector_rows = params
        normed_one = layer_norm(inputs, vector_rows[0], vector_rows[1])
        normed_two = layer_norm(inputs, vector_rows[2], vector_rows[3])
        projected = low_back(jnp.dot(low(normed_one), weight_qkv, precision=HIGHEST) + vector_rows[4:7].reshape(-1))
        query = low(rotate(projected[:, :D].reshape(LEN, HEADS, HEAD_DIM), cosines, sines))
        keys = low(rotate(projected[:, D:2 * D].reshape(LEN, HEADS, HEAD_DIM), cosines, sines))
        values = low(projected[:, 2 * D:].reshape(LEN, HEADS, HEAD_DIM))

        def one_block(arguments):
            return attend(arguments[0], arguments[1], arguments[2], keys, values, positions, pieces)
        blocks_out, block_tops = lax.map(jax.checkpoint(one_block), (query.reshape(block_count, block_rows, HEADS, HEAD_DIM), positions.reshape(block_count, block_rows), pieces.reshape(block_count, block_rows)))
        attended = low(low_back(blocks_out.reshape(LEN, D)))
        branch_attn = jnp.dot(attended, weight_out, precision=HIGHEST) + vector_rows[7]
        before = low_back(jnp.dot(low(normed_two), weight_up, precision=HIGHEST) + vector_rows[8:12].reshape(-1))
        activated = low(jax.nn.gelu(before, approximate=False))
        branch_mlp = jnp.dot(activated, weight_down, precision=HIGHEST) + vector_rows[12]
        return (inputs + branch_attn + branch_mlp, lax.optimization_barrier(jnp.max(block_tops, 0)))

    def forward(params, inputs):

        def scan_step(carried, slices):
            return (carried, one_sequence(params, slices[0], slices[1]))
        _, (outputs, peak_rows) = lax.scan(scan_step, jnp.zeros((), jnp.float32), (inputs, piece_ids))
        return (outputs, peak_rows)
    mixed, pullback, peak_rows = jax.vjp(forward, params, tokens.astype(jnp.float32), has_aux=True)
    param_grads, input_grad = pullback(cotangent.astype(jnp.float32))
    grad_qkv, grad_out, grad_up, grad_down, vector_grad = param_grads
    grad_blocks = jnp.concatenate([grad_qkv.reshape(D, 3, D).transpose(1, 0, 2), grad_out[None], grad_up.reshape(D, 4, D).transpose(1, 0, 2), grad_down.reshape(4, D, D)], 0).reshape(NB, BLOCK_ROWS, D)
    holding = (slot_block >= 0)[:, None, None]
    bank_grad = jnp.where(holding, grad_blocks[jnp.maximum(slot_block, 0)], 0.0)
    factors = clip_limit / jnp.maximum(lax.optimization_barrier(jnp.max(peak_rows, 0)), clip_limit)
    column_scale = jnp.repeat(jnp.sqrt(factors), HEAD_DIM)
    bank_new, first_new, second_new = adamw_update(master, bank_grad, first_moment, second_moment, weight_decay)
    clipped = ((slot_block >= 0) & (slot_block // (D // BLOCK_ROWS) < 2))[:, None, None]
    bank_new = jnp.where(clipped, bank_new * column_scale, bank_new)
    bank_new = jnp.where(holding, bank_new, 0.0)
    first_new = jnp.where(holding, first_new, 0.0)
    second_new = jnp.where(holding, second_new, 0.0)
    vector_new, rows_first, rows_second = adamw_update(vectors, vector_grad, vector_first, vector_second, 0.0)
    row_index = jnp.arange(13, dtype=jnp.int32)
    vector_new = jnp.where(((row_index == 4) | (row_index == 5))[:, None], vector_new * column_scale, vector_new)
    return (mixed.astype(jnp.bfloat16), input_grad, bank_grad, bank_new, first_new, second_new, vector_grad, vector_new, rows_first, rows_second, factors)
```

```python
import math

import jax
import jax.numpy as jnp
import numpy as np
from jax import lax
from jax.experimental import pallas as pl
from jax.experimental.pallas import tpu as pltpu
from jax.sharding import Mesh
from jax.sharding import PartitionSpec as P

D = 1024
HEADS = 16
HEAD_DIM = 64
FF = 4096
ROT = 16
BLOCK_ROWS = 16
PIECE = 256
GROUPS = 4
CLASSES = 3
NEG = -1e30

norm_epsilon = 1e-05
clip_limit = 4.0
beta_first = 0.9
beta_second = 0.95
learn_rate = 0.05
weight_decay = 0.1
adam_epsilon = 1e-08
adam_step = 10.0

F32 = jnp.float32
BF16 = jnp.bfloat16

CLASS_MATRICES = ((0, 1, 2, 3), (4, 5, 8, 9), (6, 7, 10, 11))


def adamw_update(weight, gradient, moment_one, moment_two, decay_rate):
    moment_one = beta_first * moment_one + (1.0 - beta_first) * gradient
    moment_two = beta_second * moment_two + (1.0 - beta_second) * gradient * gradient
    first_hat = moment_one / (1.0 - beta_first**adam_step)
    second_hat = moment_two / (1.0 - beta_second**adam_step)
    weight = weight - learn_rate * (
        first_hat / (jnp.sqrt(second_hat) + adam_epsilon) + decay_rate * weight
    )
    return (weight, moment_one, moment_two)


def norm_stats(values):
    center = values - jnp.mean(values, -1, keepdims=True)
    spread = jnp.mean(center * center, -1, keepdims=True)
    inverse = lax.rsqrt(spread + norm_epsilon)
    return center * inverse, inverse


def norm_back(grad_hat, hat, inverse):
    return inverse * (
        grad_hat
        - jnp.mean(grad_hat, -1, keepdims=True)
        - hat * jnp.mean(grad_hat * hat, -1, keepdims=True)
    )


def pick(selected, values, axes):
    return jnp.sum(jnp.where(selected, values, 0), axes)


def make_plan(owner, devices, capacity):
    blocks = owner.shape[0]
    in_class = blocks // CLASSES
    per = in_class // devices
    slots = devices * capacity
    chips = devices // 2
    pair = 2 * capacity
    block_ids = jnp.arange(blocks, dtype=jnp.int32)
    slot_ids = jnp.arange(slots, dtype=jnp.int32)
    at_slot = owner[None, :] == slot_ids[:, None]
    slot_block = jnp.max(jnp.where(at_slot, block_ids[None, :], -1), 1)
    occupied = slot_block >= 0
    matrix = jnp.maximum(slot_block, 0) // (D // BLOCK_ROWS)
    slot_class = jnp.where(matrix < 4, 0, 1 + (matrix // 2) % 2)
    class_ids = jnp.arange(CLASSES, dtype=jnp.int32)
    member = ((slot_class[None] == class_ids[:, None]) & occupied[None]).reshape(CLASSES, chips, pair)
    member_f = member.astype(F32)
    pair_ids = jnp.arange(pair)
    before = (pair_ids[:, None] < pair_ids[None, :]).astype(F32)
    rank = jnp.einsum("kcs,st->kct", member_f, before, preferred_element_type=F32).astype(jnp.int32)
    total = jnp.sum(member_f, -1).astype(jnp.int32)
    half = (total + 1) // 2
    second = rank >= half[..., None]
    place = rank - jnp.where(second, half[..., None], 0)
    count = jnp.stack([half, total - half], -1).reshape(CLASSES, devices)
    over = jnp.maximum(count - per, 0)
    free = jnp.maximum(per - count, 0)
    dev = jnp.arange(devices, dtype=jnp.int32)
    ahead = (over[:, None, :] > over[:, :, None]) | (
        (over[:, None, :] == over[:, :, None]) & (dev[None, None, :] < dev[None, :, None])
    )
    offset = jnp.sum(jnp.where(ahead, over[:, None, :], 0), -1)
    level = jnp.arange(per, dtype=jnp.int32)
    level_start = jnp.sum(jnp.minimum(free[:, :, None], level), 1)
    valid = free[:, :, None] > level
    earlier = jnp.sum(
        jnp.where(valid[:, None] & (dev[None, None, :, None] < dev[None, :, None, None]), 1, 0), 2
    )
    order = level_start[:, None, :] + earlier
    owns = (
        (order[..., None] >= offset[:, None, None, :])
        & (order[..., None] < (offset + over)[:, None, None, :])
        & valid[..., None]
    )
    source = pick(owns, dev, -1)
    extra = order - pick(owns, offset[:, None, None, :], -1)
    flat = lambda a: a.transpose(1, 0, 2).reshape(devices, CLASSES * per)
    source_f, valid_f, extra_f = flat(source), flat(valid), flat(extra)
    index_f = jnp.arange(CLASSES * per)
    same = (
        (source_f[:, :, None] == source_f[:, None, :])
        & valid_f[:, None, :]
        & (index_f[None, None, :] < index_f[None, :, None])
    )
    turn_f = jnp.sum(same.astype(jnp.int32), -1)
    rounds = jnp.max(jnp.where(valid_f, turn_f + 1, 0))
    turn = turn_f.reshape(devices, CLASSES, per).transpose(1, 0, 2)
    home_dev = 2 * jnp.arange(chips, dtype=jnp.int32)[None, :, None] + second
    offset_s = jnp.where(second, offset.reshape(CLASSES, chips, 2)[..., 1:], offset.reshape(CLASSES, chips, 2)[..., :1])
    wanted = (offset_s + place - per).reshape(CLASSES, slots)
    hole_position = dev[None, :, None] * per + count[..., None] + level
    filled = jnp.where(valid, order, -1).reshape(CLASSES, devices * per)
    moved = pick(
        wanted[:, :, None] == filled[:, None, :],
        hole_position.reshape(CLASSES, 1, devices * per),
        -1,
    )
    stays = home_dev * per + place
    position = jnp.where(place < per, stays, moved.reshape(CLASSES, chips, pair))
    position = jnp.sum(jnp.where(member, position, 0), 0).reshape(slots)
    block_position = pick(at_slot, position[:, None], 0)
    by_class = block_position[
        np.concatenate([np.arange(64) + 64 * m for ms in CLASS_MATRICES for m in ms])
    ].reshape(CLASSES, in_class)
    spots = jnp.arange(in_class, dtype=jnp.int32)
    at_position = pick(by_class[:, None, :] == spots[None, :, None], spots[None, None, :], -1)
    return dict(
        per=per, slot_block=slot_block, member=member, second=second, place=place, count=count, offset=offset,
        order=order, valid=valid, turn=turn, source_f=source_f, valid_f=valid_f, extra_f=extra_f, turn_f=turn_f,
        rounds=rounds, by_class=by_class, at_position=at_position, pair=pair, capacity=capacity, devices=devices,
    )


def local_plan(plan, me):
    per, pair, capacity, devices = plan["per"], plan["pair"], plan["capacity"], plan["devices"]
    row = lambda a, i, axis: lax.dynamic_index_in_dim(a, i, axis, keepdims=False)
    chip, mine = me // 2, me % 2
    member, second, place = (row(plan[n], chip, 1) for n in ("member", "second", "place"))
    held = member & (second.astype(jnp.int32) == mine)
    slot = jnp.arange(pair, dtype=jnp.int32)
    where_slot = jnp.where(slot // capacity == mine, slot % capacity, capacity + slot % capacity)
    spot = jnp.arange(per, dtype=jnp.int32)
    home = pick(held[:, None, :] & (place[:, None, :] == spot[None, :, None]), where_slot, -1)
    count = row(plan["count"], me, 1)
    hole = spot[None, :, None] - count[:, None, None] == spot[None, None, :]
    valid_me, turn_me = row(plan["valid"], me, 1), row(plan["turn"], me, 1)
    source_me = row(plan["source_f"], me, 0).reshape(CLASSES, per)
    hole_source = pick(hole, source_me[:, None, :], -1)
    hole_turn = jnp.sum(jnp.where(hole & valid_me[:, None, :], turn_me[:, None, :] + 1, 0), -1) - 1
    sent = plan["valid_f"] & (plan["source_f"] == me)
    class_f = jnp.repeat(jnp.arange(CLASSES, dtype=jnp.int32), per)

    def forward_index(turn):
        here = sent & (plan["turn_f"] == turn)
        kind = pick(here, class_f, -1)
        beyond = pick(here, plan["extra_f"], -1)
        match = (
            held[None]
            & (kind[:, None, None] == jnp.arange(CLASSES)[None, :, None])
            & (place[None] == per + beyond[:, None, None])
        )
        return pick(match, where_slot, (1, 2))

    spot_f = (jnp.arange(CLASSES, dtype=jnp.int32)[:, None] * per + count[:, None] + spot[None, :]).reshape(-1)
    got_f, got_turn = source_me.reshape(-1), turn_me.reshape(-1)
    got_valid = valid_me.reshape(-1)

    def backward_index(turn):
        match = (got_f[None, :] == jnp.arange(devices)[:, None]) & (got_valid & (got_turn == turn))[None, :]
        return pick(match, spot_f, -1)

    want = row(plan["offset"], me, 1)[:, None] + place - per
    match = (want[:, :, None, None] == plan["order"][:, None]) & plan["valid"][:, None]
    match = match & (held & (place >= per))[:, :, None, None]
    answer = pick(match, jnp.arange(devices, dtype=jnp.int32)[None, None, :, None], (0, 2, 3))
    answer_turn = jnp.sum(jnp.where(match, plan["turn"][:, None] + 1, 0), (0, 2, 3)) - 1
    at_home = held & (place < per)
    home_spot = pick(at_home, jnp.arange(CLASSES, dtype=jnp.int32)[:, None] * per + place, 0)
    mine_holds = jnp.any(held, 0)
    sort_pair = lambda a: jnp.where(mine == 0, a, jnp.concatenate([a[capacity:], a[:capacity]]))
    return dict(
        home=home, hole_source=hole_source, hole_turn=hole_turn, forward_index=forward_index,
        backward_index=backward_index, answer=sort_pair(answer), answer_turn=sort_pair(answer_turn),
        home_spot=sort_pair(home_spot), holds=sort_pair(mine_holds),
    )


def rotary_lanes(positions):
    halves = jnp.arange(ROT // 2, dtype=F32)
    inverse = jnp.exp(-math.log(10000.0) * 2.0 * halves / ROT)
    angles = positions[:, None] * inverse[None, :]
    cos, sin = jnp.cos(angles), jnp.sin(angles)
    rest = HEAD_DIM - ROT
    ones, zeros = jnp.ones((positions.shape[0], rest), F32), jnp.zeros((positions.shape[0], rest), F32)
    blank = jnp.zeros_like(sin)
    cos_row = jnp.concatenate([cos, cos, ones], -1)
    low_row = jnp.concatenate([-sin, blank, zeros], -1)
    high_row = jnp.concatenate([blank, sin, zeros], -1)
    return tuple(jnp.concatenate([t, t], -1) for t in (cos_row, low_row, high_row))


def turn_lanes(u, cos, low, high):
    width = u.shape[-1]
    return u * cos + pltpu.roll(u, width - ROT // 2, 1) * low + pltpu.roll(u, ROT // 2, 1) * high


def project_kernel(x_ref, e_ref, gain_ref, w_ref, wo_ref, b_ref, cos_ref, low_ref, high_ref, out_ref, h_ref):
    kind = pl.program_id(0)

    @pl.when((kind == 0) & (pl.program_id(1) == 0))
    def _():
        hat, _ = norm_stats(x_ref[...].astype(F32))
        h_ref[...] = (hat * gain_ref[0:1, :] + gain_ref[1:2, :]).astype(BF16)

    copies = out_ref.shape[-1] // 128

    @pl.when(kind < 3)
    def _():
        u = jnp.dot(h_ref[...], w_ref[0], preferred_element_type=F32) + b_ref[0]

        @pl.when(kind < 2)
        def _():
            for i in range(copies):
                lanes = slice(128 * i, 128 * (i + 1))
                out_ref[0, 0, :, lanes] = turn_lanes(
                    u[:, lanes], cos_ref[...], low_ref[...], high_ref[...]
                ).astype(BF16)

        @pl.when(kind == 2)
        def _():
            out_ref[0, 0] = u.astype(BF16)

    @pl.when(kind == 3)
    def _():
        out_ref[0, 0] = lax.dot_general(
            e_ref[...], wo_ref[0], (((1,), (1,)), ((), ())), preferred_element_type=F32
        ).astype(BF16)


def project(x, e, gains, weights, biases, tables, members):
    rows = x.shape[0]
    cols = D // members
    whole = lambda shape: pl.BlockSpec(shape, lambda k, m: (0,) * len(shape))
    return pl.pallas_call(
        project_kernel,
        grid=(4, members),
        in_specs=[
            whole((rows, D)),
            whole((rows, D)),
            whole((2, D)),
            pl.BlockSpec((1, D, cols), lambda k, m: (jnp.minimum(k, 2), 0, jnp.where(k < 3, m, members - 1))),
            pl.BlockSpec((1, cols, D), lambda k, m: (3, jnp.where(k < 3, 0, m), 0)),
            pl.BlockSpec((1, 1, cols), lambda k, m: (jnp.minimum(k, 2), 0, m)),
            whole((rows, 128)),
            whole((rows, 128)),
            whole((rows, 128)),
        ],
        out_specs=[
            pl.BlockSpec((1, 1, rows, cols), lambda k, m: (m, k, 0, 0)),
            whole((rows, D)),
        ],
        out_shape=[
            jax.ShapeDtypeStruct((members, 4, rows, cols), BF16),
            jax.ShapeDtypeStruct((rows, D), BF16),
        ],
        cost_estimate=pl.CostEstimate(
            flops=2 * rows * D * 4 * D, bytes_accessed=8 * D * D + 14 * rows * D, transcendentals=0
        ),
        name="project",
    )(x, e, gains, weights, weights, biases.reshape(3, 1, D), *tables)


def attend_kernel(
    flag_ref, mine_ref, cos_ref, low_ref, high_ref, in_ref, out_ref, top_ref,
    q_s, k_s, v_s, do_s, kt_s, vt_s, dot_s, ot_s, dqt_s, s_s, p_s, dk_s, dv_s,
):
    seq = pl.program_id(0)
    members, _, groups, _, seg, _ = in_ref.shape
    length = members * groups * seg
    mine = mine_ref[0]
    scale = HEAD_DIM**-0.5

    def row_of(j, m):
        source = jnp.bitwise_xor(mine, j)
        return pl.multiple_of((source * members + m) * seg, seg)

    lane = lax.broadcasted_iota(jnp.int32, (1, 128), 1)
    masks = [jnp.where(lane // HEAD_DIM == h, 1.0, 0.0).astype(BF16) for h in range(2)]
    for j in range(groups):
        for m in range(members):
            rows = pl.ds(row_of(j, m), seg)
            q = in_ref[m, 0, j, 0]
            do = in_ref[m, 3, j, 0]
            for h in range(2):
                q_s[h, rows, :] = q * (masks[h] * scale).astype(BF16)
                do_s[h, rows, :] = do * masks[h]
            k_s[rows, :] = in_ref[m, 1, j, 0]
            v_s[rows, :] = in_ref[m, 2, j, 0]
    kt_s[...] = k_s[...].T
    vt_s[...] = v_s[...].T
    dot_s[...] = (do_s[0] + do_s[1]).T
    dk_s[...] = jnp.zeros_like(dk_s)
    dv_s[...] = jnp.zeros_like(dv_s)
    key_index = lax.broadcasted_iota(jnp.int32, (PIECE, PIECE), 0)
    query_index = lax.broadcasted_iota(jnp.int32, (PIECE, PIECE), 1)
    causal = key_index <= query_index
    nt = (((1,), (1,)), ((), ()))

    for h in range(2):
        dims = slice(HEAD_DIM * h, HEAD_DIM * (h + 1))

        def span_step(span, peak, h=h, dims=dims):
            queries = pl.ds(pl.multiple_of(span * PIECE, PIECE), PIECE)
            q = q_s[h, queries, :]
            do = do_s[h, queries, :]
            piece = flag_ref[seq, span] > 0
            chunk = lambda c: pl.ds(pl.multiple_of(c * PIECE, PIECE), PIECE)
            fold = lambda a, op: op(a.reshape(PIECE // 8, 8, PIECE), 0)

            s = lax.dot_general(k_s[queries, :], q, nt, preferred_element_type=F32)
            s = jnp.where(causal | piece, s, NEG)
            s_s[queries, :] = s

            def score(c, top):
                s = lax.dot_general(k_s[chunk(c), :], q, nt, preferred_element_type=F32)
                s_s[chunk(c), :] = s
                return jnp.maximum(top, fold(s, jnp.max))

            top = lax.fori_loop(0, span, score, fold(s, jnp.max))
            top = jnp.max(top, 0, keepdims=True)

            def soften(c, total):
                e = jnp.exp(s_s[chunk(c), :] - top)
                s_s[chunk(c), :] = e
                return total + fold(e, jnp.sum)

            total = lax.fori_loop(0, span + 1, soften, jnp.zeros((8, PIECE), F32))
            inverse = 1.0 / jnp.sum(total, 0, keepdims=True)

            def output(c, o):
                p = s_s[chunk(c), :] * inverse
                s_s[chunk(c), :] = p
                low = p.astype(BF16)
                p_s[chunk(c), :] = low
                return o + jnp.dot(vt_s[dims, chunk(c)], low, preferred_element_type=F32)

            o = lax.fori_loop(0, span + 1, output, jnp.zeros((HEAD_DIM, PIECE), F32))
            ot_s[dims, queries] = o
            delta = jnp.sum(o * dot_s[dims, queries].astype(F32), 0, keepdims=True)

            def back(c, dq):
                keys = chunk(c)
                dp = lax.dot_general(v_s[keys, :], do, nt, preferred_element_type=F32)
                ds = (s_s[keys, :] * (dp - delta)).astype(BF16)
                dk_s[keys, :] += jnp.dot(ds, q, preferred_element_type=F32)
                dv_s[keys, :] += jnp.dot(p_s[keys, :], do, preferred_element_type=F32)
                return dq + jnp.dot(kt_s[dims, keys], ds, preferred_element_type=F32)

            dq = lax.fori_loop(0, span + 1, back, jnp.zeros((HEAD_DIM, PIECE), F32))
            dqt_s[dims, queries] = dq * scale
            return jnp.maximum(peak, top)

        peak = lax.fori_loop(0, length // PIECE, span_step, jnp.full((1, PIECE), NEG, F32))
        top_ref[0, 0, h : h + 1, :] = jnp.max(peak.reshape(2, 128), 0, keepdims=True)

    back_turn = lambda u: turn_lanes(u, cos_ref[...], -low_ref[...], -high_ref[...]).astype(BF16)
    q_s[0] = ot_s[...].T.astype(BF16)
    q_s[1] = back_turn(dqt_s[...].T)
    do_s[0] = back_turn(dk_s[...])
    do_s[1] = dv_s[...].astype(BF16)
    for j in range(groups):
        for m in range(members):
            rows = pl.ds(row_of(j, m), seg)
            out_ref[m, 0, j, 0] = q_s[0, rows, :]
            out_ref[m, 1, j, 0] = q_s[1, rows, :]
            out_ref[m, 2, j, 0] = do_s[0, rows, :]
            out_ref[m, 3, j, 0] = do_s[1, rows, :]


def attend(flags, group, tables, packed):
    members, four, groups, seqs, seg, cols = packed.shape
    length = members * groups * seg
    block = pl.BlockSpec((members, four, groups, 1, seg, 128), lambda s, h: (0, 0, 0, s, 0, h))
    table = pl.BlockSpec((length, 128), lambda s, h: (0, 0))
    smem = pl.BlockSpec(memory_space=pltpu.SMEM)
    tiles = (length // PIECE) * (length // PIECE + 1) // 2 * seqs * cols // HEAD_DIM
    return pl.pallas_call(
        attend_kernel,
        grid=(seqs, cols // 128),
        in_specs=[smem, smem, table, table, table, block],
        out_specs=[block, pl.BlockSpec((1, 1, 8, 128), lambda s, h: (s, h, 0, 0))],
        out_shape=[
            jax.ShapeDtypeStruct(packed.shape, BF16),
            jax.ShapeDtypeStruct((seqs, cols // 128, 8, 128), F32),
        ],
        scratch_shapes=[
            pltpu.VMEM((2, length, 128), BF16),
            pltpu.VMEM((length, 128), BF16),
            pltpu.VMEM((length, 128), BF16),
            pltpu.VMEM((2, length, 128), BF16),
            pltpu.VMEM((128, length), BF16),
            pltpu.VMEM((128, length), BF16),
            pltpu.VMEM((128, length), BF16),
            pltpu.VMEM((128, length), F32),
            pltpu.VMEM((128, length), F32),
            pltpu.VMEM((length, PIECE), F32),
            pltpu.VMEM((length, PIECE), BF16),
            pltpu.VMEM((length, 128), F32),
            pltpu.VMEM((length, 128), F32),
        ],
        cost_estimate=pl.CostEstimate(
            flops=tiles * 5 * 2 * PIECE * PIECE * 256, bytes_accessed=packed.size * 4, transcendentals=tiles * PIECE**2
        ),
        name="attend",
    )(flags, group, *tables, packed)


def make_body(sizes):
    dp_size, group_size, pair_size = sizes["dp"], sizes["g"], sizes["m"]
    devices = dp_size * group_size * pair_size * 2
    members = pair_size * 2
    every = ("dp", "g", "m", "c")

    def swap(value, axis, k):
        return lax.ppermute(value, axis, [(i, i ^ k) for i in range(sizes[axis])])

    def butterfly(value, combine, axes):
        for axis in axes:
            k = 1
            while k < sizes[axis]:
                value = combine(value, swap(value, axis, k))
                k *= 2
        return value

    def body(
        tokens, piece_ids, cotangent, master, first_moment, second_moment, owner_slot, vectors, vector_first, vector_second
    ):
        index = {a: lax.axis_index(a) for a in every}
        group = index["g"]
        member = index["m"] * 2 + index["c"]
        me = (index["dp"] * group_size + group) * members + member
        capacity = master.shape[0]
        batch, seg = tokens.shape[0], tokens.shape[1]
        seqs = batch // group_size
        rows = batch * seg
        order = jnp.bitwise_xor(group, jnp.arange(group_size, dtype=jnp.int32))

        def by_order(a):
            return jnp.take(a.reshape((group_size, seqs) + a.shape[1:]), order, axis=0)

        def from_order(a):
            return jnp.take(a, order, axis=0).reshape((batch,) + a.shape[2:])

        def cross(a):
            return jnp.stack([a[0]] + [swap(a[k], "g", k) for k in range(1, group_size)])

        own_tokens = by_order(tokens)
        own_cotangent = by_order(cotangent)
        there_tokens = cross(own_tokens).reshape(rows, D)
        there_cotangent = cross(own_cotangent).reshape(rows, D)
        own_tokens = own_tokens.reshape(rows, D)
        own_cotangent = own_cotangent.reshape(rows, D)
        context = group * members + member
        flags = jnp.where(
            jnp.arange(group_size * members)[:, None] == context, piece_ids[None, :, 0], 0
        ).astype(jnp.int32)
        flags = butterfly(flags, jnp.add, ("c", "m", "g"))
        span_step = PIECE // seg
        flags = lax.dynamic_slice_in_dim(flags[::span_step], group * seqs, seqs, 1).T

        plan = make_plan(owner_slot, devices, capacity)
        local = local_plan(plan, me)
        per = plan["per"]
        low_master = master.astype(BF16)
        chip_slots = jnp.concatenate([low_master, swap(low_master, "c", 1)], 0)
        held = chip_slots[local["home"].reshape(-1)].reshape(CLASSES, per, BLOCK_ROWS, D)

        def deliver(turn, held):
            send = chip_slots[local["forward_index"](turn)]
            got = lax.all_to_all(send, every, 0, 0, tiled=True)
            arrived = got[local["hole_source"].reshape(-1)].reshape(held.shape)
            return jnp.where((local["hole_turn"] == turn)[:, :, None, None], arrived, held)

        held = deliver(0, held)
        _, held = lax.while_loop(
            lambda c: c[0] < plan["rounds"], lambda c: (c[0] + 1, deliver(c[0], c[1])), (jnp.int32(1), held)
        )
        matrices = []
        for k in range(CLASSES):
            gathered = lax.all_gather(held[k], every, axis=0, tiled=True)
            matrices.append(gathered[plan["by_class"][k]].reshape(4, D, D))

        chunk_starts = (order[:, None] * members + member) * seg
        positions = (chunk_starts[:, None, :] + jnp.arange(seg)[None, None, :]) + jnp.zeros((1, seqs, 1), jnp.int32)
        own_tables = rotary_lanes(positions.reshape(rows).astype(F32))
        length = group_size * members * seg
        all_tables = rotary_lanes(jnp.arange(length, dtype=F32))
        packed, low_one = project(
            there_tokens, there_cotangent, vectors[0:2], matrices[0], vectors[4:7], own_tables, members
        )
        packed = lax.all_to_all(packed, ("m", "c"), 0, 0, tiled=True)
        packed = packed.reshape(members, 4, group_size, seqs, seg, D // members)
        back, tops = attend(flags, group.reshape(1).astype(jnp.int32), all_tables, packed)
        back = lax.all_to_all(back.reshape(members, 4, rows, D // members), ("m", "c"), 0, 0, tiled=True)
        back = back.transpose(1, 2, 0, 3).reshape(4, rows, D)
        attended, grad_proj = back[0], back[1:]

        own_f = own_tokens.astype(F32)
        hat_two, inverse_two = norm_stats(own_f)
        low_two = (hat_two * vectors[2] + vectors[3]).astype(BF16)
        branch = jnp.zeros((rows, D), F32)
        grad_two = jnp.zeros((rows, D), F32)
        up_bias = []
        block_grads = [None] * CLASSES
        for k in (1, 2):
            ups, downs = [], []
            for j in range(2):
                up, down = matrices[k][j], matrices[k][2 + j]
                before = jnp.dot(low_two, up, preferred_element_type=F32) + vectors[8 + 2 * (k - 1) + j]
                cdf = 0.5 * (1.0 + lax.erf(before * (0.5**0.5)))
                active = (before * cdf).astype(BF16)
                slope = cdf + before * jnp.exp(-0.5 * before * before) * ((2.0 * math.pi) ** -0.5)
                branch += jnp.dot(active, down, preferred_element_type=F32)
                grad_active = jnp.einsum("td,fd->tf", own_cotangent, down, preferred_element_type=F32)
                grad_before = (grad_active * slope).astype(BF16)
                up_bias.append(jnp.sum(grad_before.astype(F32), 0))
                grad_two += jnp.einsum("tf,df->td", grad_before, up, preferred_element_type=F32)
                ups.append(jnp.einsum("td,tf->df", low_two, grad_before, preferred_element_type=F32).astype(BF16))
                downs.append(jnp.einsum("tf,td->fd", active, own_cotangent, preferred_element_type=F32).astype(BF16))
            block_grads[k] = jnp.stack(ups + downs)

        grad_out = jnp.einsum("te,td->ed", attended, there_cotangent, preferred_element_type=F32).astype(BF16)
        grad_qkv = [
            jnp.einsum("td,te->de", low_one, grad_proj[j], preferred_element_type=F32).astype(BF16) for j in range(3)
        ]
        block_grads[0] = jnp.stack(grad_qkv + [grad_out])
        grad_one = sum(
            jnp.einsum("te,de->td", grad_proj[j], matrices[0][j], preferred_element_type=F32) for j in range(3)
        )
        hat_one, inverse_one = norm_stats(there_tokens.astype(F32))
        input_one = norm_back(grad_one * vectors[0], hat_one, inverse_one).astype(BF16)
        attended_home = cross(attended.reshape(group_size, seqs, seg, D)).reshape(rows, D)
        input_one_home = cross(input_one.reshape(group_size, seqs, seg, D)).reshape(rows, D)
        branch_attn = jnp.dot(attended_home, matrices[0][3], preferred_element_type=F32) + vectors[7]
        mixed = (own_f + branch_attn + branch + vectors[12]).astype(BF16)
        input_two = norm_back(grad_two * vectors[2], hat_two, inverse_two)
        wide = own_cotangent.astype(F32)
        input_grad = wide + input_two + input_one_home.astype(F32)
        shape4 = (group_size, seqs, seg, D)
        mixed = from_order(mixed.reshape(shape4))
        input_grad = from_order(input_grad.reshape(shape4))

        wide_sum = jnp.sum(wide, 0)
        proj_sum = jnp.sum(grad_proj.astype(F32), 1)
        peaks = jnp.max(tops[:, :, :2], (0, 3)).reshape(-1)
        heads_here = HEADS // members
        peak_row = jnp.full((D,), NEG, F32)
        peak_row = lax.dynamic_update_slice(peak_row, peaks, (member * heads_here,))
        small = jnp.concatenate(
            [
                jnp.stack(
                    [
                        jnp.sum(grad_one * hat_one, 0),
                        jnp.sum(grad_one, 0),
                        jnp.sum(grad_two * hat_two, 0),
                        jnp.sum(grad_two, 0),
                    ]
                ),
                proj_sum,
                wide_sum[None],
                jnp.stack(up_bias),
                wide_sum[None],
                peak_row[None],
            ],
            0,
        )
        is_peak = (jnp.arange(14) == 13)[:, None]
        small = butterfly(small, lambda a, b: jnp.where(is_peak, jnp.maximum(a, b), a + b), ("c", "m", "dp", "g"))
        vector_sum, overall_peak = small[:13], small[13, :HEADS]

        def scatter_sum(value, axes):
            names = list(every)
            for axis in axes:
                at = names.index(axis)
                take = lambda i: lax.dynamic_index_in_dim(value, i, at, keepdims=False)
                total = take(index[axis]).astype(F32)
                for k in range(1, sizes[axis]):
                    sent = take(jnp.bitwise_xor(index[axis], k)).astype(BF16)
                    total = total + swap(sent, axis, k).astype(F32)
                value = total
                names.remove(axis)
            return value

        sums = []
        cut = per // 2
        for k in range(CLASSES):
            placed = block_grads[k].reshape(-1, BLOCK_ROWS, D)[plan["at_position"][k]]
            placed = placed.reshape(dp_size, group_size, pair_size, 2, per, BLOCK_ROWS, D)
            parts = [scatter_sum(placed[..., cut:, :, :], ("c", "dp", "m", "g"))]
            if cut:
                parts.insert(0, scatter_sum(placed[..., :cut, :, :], ("c", "m", "dp", "g")))
            sums.append(jnp.concatenate(parts, 0))
        sums = jnp.concatenate(sums, 0)

        low_sums = sums.astype(BF16)

        def give_back(turn, chip_grads):
            got = lax.all_to_all(low_sums[local["backward_index"](turn)], every, 0, 0, tiled=True)
            arrived = got[local["answer"]].astype(F32)
            return jnp.where((local["answer_turn"] == turn)[:, None, None], arrived, chip_grads)

        chip_grads = give_back(0, sums[local["home_spot"]])
        _, chip_grads = lax.while_loop(
            lambda c: c[0] < plan["rounds"], lambda c: (c[0] + 1, give_back(c[0], c[1])), (jnp.int32(1), chip_grads)
        )
        from_sibling = swap(chip_grads[capacity:], "c", 1)
        owned = jnp.where(local["holds"][:capacity, None, None], chip_grads[:capacity], from_sibling)
        local_block = lax.dynamic_slice_in_dim(plan["slot_block"], me * capacity, capacity)
        holding = (local_block >= 0)[:, None, None]
        owned = jnp.where(holding, owned, 0.0)

        factors = clip_limit / jnp.maximum(overall_peak, clip_limit)
        column_scale = jnp.repeat(jnp.sqrt(factors), HEAD_DIM)
        clipped = ((local_block >= 0) & (local_block // (D // BLOCK_ROWS) < 2))[:, None, None]
        bank_new, first_new, second_new = adamw_update(master, owned, first_moment, second_moment, weight_decay)
        bank_new = jnp.where(clipped, bank_new * column_scale, bank_new)
        bank_new = jnp.where(holding, bank_new, 0.0)
        first_new = jnp.where(holding, first_new, 0.0)
        second_new = jnp.where(holding, second_new, 0.0)
        vector_new, rows_first, rows_second = adamw_update(vectors, vector_sum, vector_first, vector_second, 0.0)
        row_index = jnp.arange(13, dtype=jnp.int32)
        vector_new = jnp.where(
            ((row_index == 4) | (row_index == 5))[:, None], vector_new * column_scale, vector_new
        )
        return (
            mixed, input_grad, owned, bank_new, first_new, second_new, vector_sum, vector_new, rows_first, rows_second, factors,
        )

    return body


def solution(mesh):
    dp_size, ctx_size = mesh.shape["dp"], mesh.shape["ctx"]
    fine = Mesh(
        mesh.devices.reshape(dp_size, GROUPS, ctx_size // GROUPS // 2, 2), ("dp", "g", "m", "c")
    )
    ctx = ("g", "m", "c")
    slots = P(("dp",) + ctx, None, None)
    wide = P("dp", ctx, None)
    in_specs = (wide, P("dp", ctx), wide, slots, slots, slots, P(), P(), P(), P())
    out_specs = (wide, wide, slots, slots, slots, slots, P(), P(), P(), P(), P())
    return jax.shard_map(
        make_body(dict(fine.shape)), mesh=fine, in_specs=in_specs, out_specs=out_specs, check_vma=False
    )
```

```python
import math

import jax
import jax.numpy as jnp
import numpy as np
from jax import lax
from jax.experimental import pallas as pl
from jax.experimental.pallas import tpu as pltpu
from jax.sharding import Mesh
from jax.sharding import PartitionSpec as P

D = 1024
HEADS = 16
HEAD_DIM = 64
FF = 4096
ROT = 16
BLOCK_ROWS = 16
PIECE = 256
GROUPS = 4
CLASSES = 2
NEG = -1e30

norm_epsilon = 1e-05
clip_limit = 4.0
beta_first = 0.9
beta_second = 0.95
learn_rate = 0.05
weight_decay = 0.1
adam_epsilon = 1e-08
adam_step = 10.0

F32 = jnp.float32
BF16 = jnp.bfloat16

CLASS_MATRICES = ((0, 1, 2, 3), (4, 5, 6, 7, 8, 9, 10, 11))


def adamw_update(weight, gradient, moment_one, moment_two, decay_rate):
    moment_one = beta_first * moment_one + (1.0 - beta_first) * gradient
    moment_two = beta_second * moment_two + (1.0 - beta_second) * gradient * gradient
    first_hat = moment_one / (1.0 - beta_first**adam_step)
    second_hat = moment_two / (1.0 - beta_second**adam_step)
    weight = weight - learn_rate * (
        first_hat / (jnp.sqrt(second_hat) + adam_epsilon) + decay_rate * weight
    )
    return (weight, moment_one, moment_two)


def norm_stats(values):
    center = values - jnp.mean(values, -1, keepdims=True)
    spread = jnp.mean(center * center, -1, keepdims=True)
    inverse = lax.rsqrt(spread + norm_epsilon)
    return center * inverse, inverse


def norm_back(grad_hat, hat, inverse):
    return inverse * (
        grad_hat
        - jnp.mean(grad_hat, -1, keepdims=True)
        - hat * jnp.mean(grad_hat * hat, -1, keepdims=True)
    )


def pick(selected, values, axes):
    return jnp.sum(jnp.where(selected, values, 0), axes)


def make_plan(owner, devices, capacity):
    blocks = owner.shape[0]
    sizes = [64 * len(c) for c in CLASS_MATRICES]
    pers = [size // devices for size in sizes]
    most = max(pers)
    per = jnp.asarray(pers, jnp.int32)
    slots = devices * capacity
    chips = devices // 2
    pair = 2 * capacity
    i32 = lambda n: jnp.arange(n, dtype=jnp.int32)
    at_slot = owner[None, :] == i32(slots)[:, None]
    slot_block = jnp.max(jnp.where(at_slot, i32(blocks)[None, :], -1), 1)
    slot_class = jnp.where(slot_block < 0, -1, jnp.where(slot_block < sizes[0], 0, 1))
    member = (slot_class[None] == i32(CLASSES)[:, None]).reshape(CLASSES, chips, pair)
    member_f = member.astype(F32)
    before = (i32(pair)[:, None] < i32(pair)[None, :]).astype(F32)
    rank = jnp.einsum("kcs,st->kct", member_f, before, preferred_element_type=F32).astype(jnp.int32)
    total = jnp.sum(member_f, -1).astype(jnp.int32)
    half = (total + 1) // 2
    second = rank >= half[..., None]
    place = rank - jnp.where(second, half[..., None], 0)
    count = jnp.stack([half, total - half], -1).reshape(CLASSES, devices)
    over = jnp.maximum(count - per[:, None], 0)
    free = jnp.maximum(per[:, None] - count, 0)
    dev = i32(devices)
    ahead = (over[:, None, :] > over[:, :, None]) | (
        (over[:, None, :] == over[:, :, None]) & (dev[None, None, :] < dev[None, :, None])
    )
    offset = jnp.sum(jnp.where(ahead, over[:, None, :], 0), -1)
    level = i32(most)
    level_start = jnp.sum(jnp.minimum(free[:, :, None], level), 1)
    valid = free[:, :, None] > level
    key = (dev[None, :] + (devices // 2) * i32(CLASSES)[:, None]) % devices
    sooner = key[:, None, :] < key[:, :, None]
    earlier = jnp.sum((sooner[..., None] & valid[:, None]).astype(jnp.int32), 2)
    order = level_start[:, None, :] + earlier
    owns = (
        (order[..., None] >= offset[:, None, None, :])
        & (order[..., None] < (offset + over)[:, None, None, :])
        & valid[..., None]
    )
    source = pick(owns, dev, -1)
    flat = lambda a: a.transpose(1, 0, 2).reshape(devices, CLASSES * most)
    source_f, valid_f = flat(source), flat(valid)
    extra_f = flat(order - pick(owns, offset[:, None, None, :], -1))
    index_f = i32(CLASSES * most)
    same = (
        (source_f[:, :, None] // 2 == source_f[:, None, :] // 2)
        & valid_f[:, None, :]
        & (index_f[None, :] < index_f[:, None])
    )
    turn_f = jnp.sum(same.astype(jnp.int32), -1)
    rounds = jnp.max(jnp.where(valid_f, turn_f // 2 + 1, 0))
    turn = turn_f.reshape(devices, CLASSES, most).transpose(1, 0, 2)
    home_dev = 2 * i32(chips)[None, :, None] + second
    halves = offset.reshape(CLASSES, chips, 2)
    offset_s = jnp.where(second, halves[..., 1:], halves[..., :1])
    per_s = per[:, None, None]
    wanted = (offset_s + place - per_s).reshape(CLASSES, slots)
    hole_position = dev[None, :, None] * per_s + count[..., None] + level
    filled = jnp.where(valid, order, -1).reshape(CLASSES, devices * most)
    moved = pick(
        wanted[:, :, None] == filled[:, None, :],
        hole_position.reshape(CLASSES, 1, devices * most),
        -1,
    )
    position = jnp.where(place < per_s, home_dev * per_s + place, moved.reshape(CLASSES, chips, pair))
    position = jnp.sum(jnp.where(member, position, 0), 0).reshape(slots)
    block_position = pick(at_slot, position[:, None], 0)
    by_class, at_position, first = [], [], 0
    for size in sizes:
        mine = block_position[first : first + size]
        by_class.append(mine)
        at_position.append(pick(mine[:, None] == i32(size)[None, :], i32(size)[:, None], 0))
        first += size
    return dict(
        pers=pers, per=per, most=most, slot_block=slot_block, member=member, second=second, place=place, count=count,
        offset=offset, order=order, valid=valid, turn=turn, source_f=source_f, valid_f=valid_f, extra_f=extra_f,
        turn_f=turn_f, rounds=rounds, by_class=by_class, at_position=at_position, pair=pair, capacity=capacity,
        devices=devices,
    )


def local_plan(plan, me):
    pers, most, pair, capacity, devices = (plan[n] for n in ("pers", "most", "pair", "capacity", "devices"))
    per = plan["per"][:, None]
    row = lambda a, i, axis: lax.dynamic_index_in_dim(a, i, axis, keepdims=False)
    i32 = lambda n: jnp.arange(n, dtype=jnp.int32)
    chip, mine = me // 2, me % 2
    member, second, place = (row(plan[n], chip, 1) for n in ("member", "second", "place"))
    held = member & (second.astype(jnp.int32) == mine)
    slot = i32(pair)
    where_slot = jnp.where(slot // capacity == mine, slot % capacity, capacity + slot % capacity)
    spot = i32(most)
    home = pick(held[:, None, :] & (place[:, None, :] == spot[None, :, None]), where_slot, -1)
    count = row(plan["count"], me, 1)
    hole = spot[None, :, None] - count[:, None, None] == spot[None, None, :]
    valid_me, turn_me = row(plan["valid"], me, 1), row(plan["turn"], me, 1)
    source_me = row(plan["source_f"], me, 0).reshape(CLASSES, most)
    hole_from = pick(hole, (source_me // 2 * 2 + turn_me % 2)[:, None, :], -1)
    hole_round = jnp.sum(jnp.where(hole & valid_me[:, None, :], turn_me[:, None, :] // 2 + 1, 0), -1) - 1
    flat = lambda a: jnp.concatenate([a[k, :p] for k, p in enumerate(pers)])
    sent = plan["valid_f"] & (plan["source_f"] // 2 == chip) & (plan["turn_f"] % 2 == mine)
    class_f = jnp.repeat(i32(CLASSES), most)
    beyond_slot = jnp.where(member, 2 * (place - per) + second, -1)

    def forward_index(turn):
        here = sent & (plan["turn_f"] // 2 == turn)
        kind = jnp.where(jnp.any(here, -1), pick(here, class_f, -1), CLASSES)
        beyond = pick(here, 2 * plan["extra_f"] + plan["source_f"] % 2, -1)
        match = (kind[:, None, None] == i32(CLASSES)[None, :, None]) & (beyond_slot[None] == beyond[:, None, None])
        return pick(match, where_slot, (1, 2))

    first = np.cumsum([0] + pers[:-1]).astype(np.int32)[:, None]
    spot_f = (first + count[:, None] + spot[None, :]).reshape(-1)
    back_to = jnp.where(valid_me, source_me // 2 * 2 + turn_me % 2, -1).reshape(-1)
    back_round = (turn_me // 2).reshape(-1)

    def backward_index(turn):
        match = (back_to[None, :] == i32(devices)[:, None]) & (back_round == turn)[None, :]
        return pick(match, spot_f, -1)

    beyond = member & (place >= per)
    offsets = row(plan["offset"].reshape(CLASSES, devices // 2, 2), chip, 1)
    want = jnp.where(beyond, jnp.where(second, offsets[:, 1:], offsets[:, :1]) + place - per, -1)
    filled = jnp.where(plan["valid"], plan["order"], -2).reshape(CLASSES, 1, -1)
    match = want[:, :, None] == filled
    code = plan["turn"] * devices + i32(devices)[None, :, None]
    code = pick(match, code.reshape(CLASSES, 1, -1), (0, 2))
    beyond = jnp.any(beyond, 0)
    answer = code % devices
    answer_turn = code // devices
    answer_round = jnp.where(beyond & (answer_turn % 2 == mine), answer_turn // 2, -1)
    home_spot = pick(member & (place < per), first + place, 0)
    holds = jnp.where(beyond, answer_turn % 2 == mine, jnp.any(held, 0))
    sort_pair = lambda a: jnp.where(mine == 0, a, jnp.concatenate([a[capacity:], a[:capacity]]))
    return dict(
        home=flat(home), hole_from=flat(hole_from), hole_round=flat(hole_round), forward_index=forward_index,
        backward_index=backward_index, answer=sort_pair(answer), answer_round=sort_pair(answer_round),
        home_spot=sort_pair(home_spot), holds=sort_pair(holds),
    )


def rotary_lanes(positions):
    halves = jnp.arange(ROT // 2, dtype=F32)
    inverse = jnp.exp(-math.log(10000.0) * 2.0 * halves / ROT)
    angles = positions[:, None] * inverse[None, :]
    cos, sin = jnp.cos(angles), jnp.sin(angles)
    rest = HEAD_DIM - ROT
    ones, zeros = jnp.ones((positions.shape[0], rest), F32), jnp.zeros((positions.shape[0], rest), F32)
    blank = jnp.zeros_like(sin)
    cos_row = jnp.concatenate([cos, cos, ones], -1)
    low_row = jnp.concatenate([-sin, blank, zeros], -1)
    high_row = jnp.concatenate([blank, sin, zeros], -1)
    return tuple(jnp.concatenate([t, t], -1) for t in (cos_row, low_row, high_row))


def turn_lanes(u, cos, low, high):
    width = u.shape[-1]
    return u * cos + pltpu.roll(u, width - ROT // 2, 1) * low + pltpu.roll(u, ROT // 2, 1) * high


def fetch_blocks(index_ref, first, count, blocks_ref, matrix_ref, sem):
    @pl.loop(0, count)
    def _(i):
        rows = pl.ds(pl.multiple_of(i * BLOCK_ROWS, BLOCK_ROWS), BLOCK_ROWS)
        pltpu.make_async_copy(blocks_ref.at[index_ref[first + i]], matrix_ref.at[rows], sem).start()


def wait_blocks(matrix_ref, sem):
    pltpu.make_async_copy(matrix_ref, matrix_ref, sem).wait()


def store_blocks(index_ref, first, count, matrix_ref, keep_ref, send_ref, sem):
    half = keep_ref.shape[0]

    @pl.loop(0, count)
    def _(i):
        rows = pl.ds(pl.multiple_of(i * BLOCK_ROWS, BLOCK_ROWS), BLOCK_ROWS)
        to = index_ref[first + i]

        @pl.when(to < half)
        def _():
            pltpu.make_async_copy(matrix_ref.at[rows], keep_ref.at[to], sem).start()

        @pl.when(to >= half)
        def _():
            pltpu.make_async_copy(matrix_ref.at[rows], send_ref.at[to - half], sem).start()


IN_MATRIX = D // BLOCK_ROWS
NT = (((1,), (1,)), ((), ()))
TILE = 256


def project_kernel(index_ref, x_ref, e_ref, gain_ref, b_ref, cos_ref, low_ref, high_ref, blocks_ref, *refs):
    *out_refs, h_ref, w_s, sems = refs
    kind = pl.program_id(0)
    slot = kind % 2
    part = out_refs[0].shape[2]
    members, cols = out_refs[0].shape[0], out_refs[0].shape[3]

    @pl.when(kind == 0)
    def _():
        fetch_blocks(index_ref, 0, IN_MATRIX, blocks_ref, w_s.at[0], sems.at[0])
        for i in range(len(out_refs)):
            rows = slice(part * i, part * (i + 1))
            hat, _ = norm_stats(x_ref[rows, :].astype(F32))
            h_ref[rows, :] = (hat * gain_ref[0:1, :] + gain_ref[1:2, :]).astype(BF16)

    wait_blocks(w_s.at[slot], sems.at[slot])

    @pl.when(kind < 3)
    def _():
        fetch_blocks(index_ref, (kind + 1) * IN_MATRIX, IN_MATRIX, blocks_ref, w_s.at[1 - slot], sems.at[1 - slot])

    for i, out_ref in enumerate(out_refs):
        rows = slice(part * i, part * (i + 1))
        for m in range(members):
            lanes = slice(cols * m, cols * (m + 1))

            @pl.when(kind < 3)
            def _(out_ref=out_ref, rows=rows, lanes=lanes, m=m):
                u = jnp.dot(h_ref[rows, :], w_s[slot, :, lanes], preferred_element_type=F32) + b_ref[0, :, lanes]
                turned = [
                    turn_lanes(u[:, 128 * j : 128 * (j + 1)], cos_ref[0], low_ref[0], high_ref[0])
                    for j in range(cols // 128)
                ]
                out_ref[m, 0] = jnp.concatenate(turned, 1).astype(BF16)

            @pl.when(kind == 3)
            def _(out_ref=out_ref, rows=rows, lanes=lanes, m=m):
                out_ref[m, 0] = lax.dot_general(
                    e_ref[rows, :], w_s[slot, lanes, :], NT, preferred_element_type=F32
                ).astype(BF16)


def project(index, x, e, gains, blocks, biases, tables, members, seqs):
    rows = x.shape[0]
    part = rows // seqs
    cols = D // members
    whole = lambda shape: pl.BlockSpec(shape, lambda k: (0,) * len(shape))
    once = lambda shape: pl.BlockSpec(shape, lambda k: (0,) * len(shape), pipeline_mode=pl.Buffered(1))
    table = pl.BlockSpec((1, part, 128), lambda k: (jnp.where(k < 2, 0, 1), 0, 0))
    return pl.pallas_call(
        project_kernel,
        grid=(4,),
        in_specs=[
            pl.BlockSpec(memory_space=pltpu.SMEM),
            once((rows, D)),
            once((rows, D)),
            whole((2, D)),
            pl.BlockSpec((1, 1, D), lambda k: (jnp.minimum(k, 2), 0, 0)),
            table,
            table,
            table,
            pl.BlockSpec(memory_space=pl.ANY),
        ],
        out_specs=[pl.BlockSpec((members, 1, part, cols), lambda k: (0, k, 0, 0))] * seqs + [whole((rows, D))],
        out_shape=[jax.ShapeDtypeStruct((members, 4, part, cols), BF16)] * seqs
        + [jax.ShapeDtypeStruct((rows, D), BF16)],
        scratch_shapes=[pltpu.VMEM((2, D, D), BF16), pltpu.SemaphoreType.DMA((2,))],
        cost_estimate=pl.CostEstimate(
            flops=2 * rows * D * 4 * D, bytes_accessed=8 * D * D + 14 * rows * D, transcendentals=0
        ),
        name="project",
    )(index, x, e, gains, biases.reshape(3, 1, D), *tables, blocks)


def mlp_kernel(
    index_ref, to_ref, x_ref, e_ref, gain_ref, b_ref, last_ref, blocks_ref,
    mixed_ref, input_ref, small_ref, keep_ref, send_ref,
    h_s, ht_s, up_s, down_s, act_s, pre_s, back_s, stage_u, stage_d, in_sems, out_sems,
):
    step, steps = pl.program_id(0), pl.num_programs(0)
    slot = step % 2
    rows_all = x_ref.shape[0]
    tiles = rows_all // TILE

    def fetch(j, slot):
        fetch_blocks(index_ref, j * IN_MATRIX, IN_MATRIX, blocks_ref, up_s.at[slot], in_sems.at[slot])
        fetch_blocks(index_ref, (steps + j) * IN_MATRIX, IN_MATRIX, blocks_ref, down_s.at[slot], in_sems.at[2 + slot])

    @pl.when(step == 0)
    def _():
        fetch(0, 0)

        @pl.loop(0, tiles)
        def _(t):
            rows = pl.ds(pl.multiple_of(t * TILE, TILE), TILE)
            x = x_ref[rows, :].astype(F32)
            hat, _ = norm_stats(x)
            h_s[rows, :] = (hat * gain_ref[0:1, :] + gain_ref[1:2, :]).astype(BF16)
            mixed_ref[rows, :] = x + last_ref[...]
            back_s[rows, :] = jnp.zeros((TILE, D), F32)

        ht_s[...] = h_s[...].T
        small_ref[...] = jnp.zeros_like(small_ref)

    wait_blocks(up_s.at[slot], in_sems.at[slot])
    wait_blocks(down_s.at[slot], in_sems.at[2 + slot])

    @pl.when(step + 1 < steps)
    def _():
        fetch(step + 1, 1 - slot)

    up, down = up_s.at[slot], down_s.at[slot]

    @pl.loop(0, tiles)
    def _(t):
        rows = pl.ds(pl.multiple_of(t * TILE, TILE), TILE)
        h, e = h_s[rows, :], e_ref[rows, :]
        for c in range(D // TILE):
            lanes = slice(TILE * c, TILE * (c + 1))
            before = jnp.dot(h, up[:, lanes], preferred_element_type=F32) + b_ref[0, :, lanes]
            grad = lax.dot_general(e, down[lanes, :], NT, preferred_element_type=F32)
            cdf = 0.5 * (1.0 + lax.erf(before * (0.5**0.5)))
            act_s[rows, lanes] = (before * cdf).astype(BF16)
            slope = cdf + before * jnp.exp(-0.5 * before * before) * ((2.0 * math.pi) ** -0.5)
            pre = (grad * slope).astype(BF16)
            pre_s[rows, lanes] = pre
            total = jnp.sum(pre.astype(F32), 0, keepdims=True)
            small_ref[pl.ds(step, 1), lanes] += total
        act, pre = act_s[rows, :], pre_s[rows, :]
        for c in range(D // TILE):
            lanes = slice(TILE * c, TILE * (c + 1))
            mixed_ref[rows, lanes] += jnp.dot(act, down[:, lanes], preferred_element_type=F32)
            back_s[rows, lanes] += lax.dot_general(pre, up[lanes, :], NT, preferred_element_type=F32)

    @pl.when(step > 0)
    def _():
        wait_blocks(stage_u, out_sems.at[0])
        wait_blocks(stage_d, out_sems.at[1])

    @pl.loop(0, D // TILE)
    def _(t):
        rows = pl.ds(pl.multiple_of(t * TILE, TILE), TILE)
        stage_u[rows, :] = jnp.dot(ht_s[rows, :], pre_s[...], preferred_element_type=F32).astype(BF16)

    store_blocks(to_ref, step * IN_MATRIX, IN_MATRIX, stage_u, keep_ref, send_ref, out_sems.at[0])

    for c in range(D // TILE):
        rows = slice(TILE * c, TILE * (c + 1))
        stage_d[rows, :] = jnp.dot(act_s[:, rows].T, e_ref[...], preferred_element_type=F32).astype(BF16)
    store_blocks(to_ref, (steps + step) * IN_MATRIX, IN_MATRIX, stage_d, keep_ref, send_ref, out_sems.at[1])

    @pl.when(step == steps - 1)
    def _():
        @pl.loop(0, tiles)
        def _(t):
            rows = pl.ds(pl.multiple_of(t * TILE, TILE), TILE)
            hat, inverse = norm_stats(x_ref[rows, :].astype(F32))
            back = back_s[rows, :]
            e = e_ref[rows, :].astype(F32)
            input_ref[rows, :] = e + norm_back(back * gain_ref[0:1, :], hat, inverse)
            small_ref[4:5, :] += jnp.sum(back * hat, 0, keepdims=True)
            small_ref[5:6, :] += jnp.sum(back, 0, keepdims=True)
            small_ref[6:7, :] += jnp.sum(e, 0, keepdims=True)

        wait_blocks(stage_u, out_sems.at[0])
        wait_blocks(stage_d, out_sems.at[1])


def mlp(index, to, x, e, gains, biases, last, blocks):
    rows = x.shape[0]
    steps = biases.shape[0]
    half = blocks.shape[0] // 2
    whole = lambda shape: pl.BlockSpec(shape, lambda k: (0,) * len(shape), pipeline_mode=pl.Buffered(1))
    smem = pl.BlockSpec(memory_space=pltpu.SMEM)
    hbm = pl.BlockSpec(memory_space=pl.ANY)
    halves = jax.ShapeDtypeStruct((half, BLOCK_ROWS, D), BF16)
    return pl.pallas_call(
        mlp_kernel,
        grid=(steps,),
        in_specs=[
            smem, smem, whole((rows, D)), whole((rows, D)), whole((2, D)),
            pl.BlockSpec((1, 1, D), lambda k: (k, 0, 0)), whole((1, D)), hbm,
        ],
        out_specs=[
            pl.BlockSpec((rows, D), lambda k: (0, 0)),
            pl.BlockSpec((rows, D), lambda k: (0, 0)),
            pl.BlockSpec((8, D), lambda k: (0, 0)),
            hbm,
            hbm,
        ],
        out_shape=[
            jax.ShapeDtypeStruct((rows, D), F32), jax.ShapeDtypeStruct((rows, D), F32),
            jax.ShapeDtypeStruct((8, D), F32), halves, halves,
        ],
        scratch_shapes=[
            pltpu.VMEM((rows, D), BF16),
            pltpu.VMEM((D, rows), BF16),
            pltpu.VMEM((2, D, D), BF16),
            pltpu.VMEM((2, D, D), BF16),
            pltpu.VMEM((rows, D), BF16),
            pltpu.VMEM((rows, D), BF16),
            pltpu.VMEM((rows, D), F32),
            pltpu.VMEM((D, D), BF16),
            pltpu.VMEM((D, D), BF16),
            pltpu.SemaphoreType.DMA((4,)),
            pltpu.SemaphoreType.DMA((2,)),
        ],
        cost_estimate=pl.CostEstimate(
            flops=12 * rows * D * FF, bytes_accessed=8 * D * FF + 12 * rows * D, transcendentals=2 * rows * FF
        ),
        name="mlp",
    )(index, to, x, e, gains, biases.reshape(steps, 1, D), last, blocks)


def rest_kernel(
    index_ref, to_ref, x_ref, e_ref, h_ref, gain_ref, back_ref, blocks_ref,
    input_ref, o_ref, small_ref, keep_ref, send_ref,
    ht_s, w_s, grad_s, sum_s, stage_s, in_sems, out_sems,
):
    step = pl.program_id(0)
    slot = step % 2
    members, cols = back_ref.shape[0], back_ref.shape[3]
    tiles = x_ref.shape[0] // TILE

    @pl.when(step == 0)
    def _():
        fetch_blocks(index_ref, 0, IN_MATRIX, blocks_ref, w_s.at[0], in_sems.at[0])
        ht_s[...] = h_ref[...].T
        sum_s[...] = jnp.zeros_like(sum_s)
        small_ref[...] = jnp.zeros_like(small_ref)

    @pl.when(step < 2)
    def _():
        fetch_blocks(index_ref, (step + 1) * IN_MATRIX, IN_MATRIX, blocks_ref, w_s.at[1 - slot], in_sems.at[1 - slot])

    for m in range(members):
        grad_s[:, cols * m : cols * (m + 1)] = back_ref[m, 0]

    @pl.when(step > 1)
    def _():
        wait_blocks(stage_s.at[slot], out_sems.at[slot])

    @pl.when(step < 3)
    def _():
        wait_blocks(w_s.at[slot], in_sems.at[slot])

        @pl.loop(0, D // TILE)
        def _(t):
            rows = pl.ds(pl.multiple_of(t * TILE, TILE), TILE)
            stage_s[slot, rows, :] = jnp.dot(ht_s[rows, :], grad_s[...], preferred_element_type=F32).astype(BF16)

        @pl.loop(0, tiles)
        def _(t):
            rows = pl.ds(pl.multiple_of(t * TILE, TILE), TILE)
            grad = grad_s[rows, :]
            small_ref[pl.ds(step, 1), :] += jnp.sum(grad.astype(F32), 0, keepdims=True)
            for c in range(D // TILE):
                lanes = slice(TILE * c, TILE * (c + 1))
                sum_s[rows, lanes] += lax.dot_general(grad, w_s[slot, lanes, :], NT, preferred_element_type=F32)

    @pl.when(step == 3)
    def _():
        o_ref[...] = grad_s[...]
        for c in range(D // TILE):
            rows = slice(TILE * c, TILE * (c + 1))
            stage_s[slot, rows, :] = jnp.dot(
                grad_s[:, rows].T, e_ref[...], preferred_element_type=F32
            ).astype(BF16)

    store_blocks(to_ref, step * IN_MATRIX, IN_MATRIX, stage_s.at[slot], keep_ref, send_ref, out_sems.at[slot])

    @pl.when(step == 3)
    def _():
        @pl.loop(0, tiles)
        def _(t):
            rows = pl.ds(pl.multiple_of(t * TILE, TILE), TILE)
            hat, inverse = norm_stats(x_ref[rows, :].astype(F32))
            grad = sum_s[rows, :]
            input_ref[rows, :] = norm_back(grad * gain_ref[0:1, :], hat, inverse).astype(BF16)
            small_ref[3:4, :] += jnp.sum(grad * hat, 0, keepdims=True)
            small_ref[4:5, :] += jnp.sum(grad, 0, keepdims=True)

        wait_blocks(stage_s.at[0], out_sems.at[0])
        wait_blocks(stage_s.at[1], out_sems.at[1])


def rest(index, to, x, e, h, gains, back, blocks):
    rows = x.shape[0]
    members, _, _, cols = back.shape
    half = blocks.shape[0] // 2
    once = lambda shape: pl.BlockSpec(shape, lambda k: (0,) * len(shape), pipeline_mode=pl.Buffered(1))
    whole = lambda shape: pl.BlockSpec(shape, lambda k: (0,) * len(shape))
    smem = pl.BlockSpec(memory_space=pltpu.SMEM)
    hbm = pl.BlockSpec(memory_space=pl.ANY)
    halves = jax.ShapeDtypeStruct((half, BLOCK_ROWS, D), BF16)
    return pl.pallas_call(
        rest_kernel,
        grid=(4,),
        in_specs=[
            smem, smem, once((rows, D)), once((rows, D)), once((rows, D)), once((2, D)),
            pl.BlockSpec((members, 1, rows, cols), lambda k: (0, (k + 1) % 4, 0, 0)), hbm,
        ],
        out_specs=[whole((rows, D)), whole((rows, D)), whole((8, D)), hbm, hbm],
        out_shape=[
            jax.ShapeDtypeStruct((rows, D), BF16), jax.ShapeDtypeStruct((rows, D), BF16),
            jax.ShapeDtypeStruct((8, D), F32), halves, halves,
        ],
        scratch_shapes=[
            pltpu.VMEM((D, rows), BF16),
            pltpu.VMEM((2, D, D), BF16),
            pltpu.VMEM((rows, D), BF16),
            pltpu.VMEM((rows, D), F32),
            pltpu.VMEM((2, D, D), BF16),
            pltpu.SemaphoreType.DMA((2,)),
            pltpu.SemaphoreType.DMA((2,)),
        ],
        cost_estimate=pl.CostEstimate(
            flops=14 * rows * D * D, bytes_accessed=14 * D * D + 20 * rows * D, transcendentals=0
        ),
        name="rest",
    )(index, to, x, e, h, gains, back, blocks)


def attend_kernel(
    flag_ref, mine_ref, cos_ref, low_ref, high_ref, in_ref, out_ref, top_ref,
    q_s, k_s, v_s, do_s, kt_s, vt_s, ot_s, dqt_s, s_s, dp_s, dk_s, dv_s,
):
    members, _, groups, seg, _ = in_ref.shape
    length = members * groups * seg
    mine = mine_ref[0]
    scale = HEAD_DIM**-0.5

    def row_of(j, m):
        source = jnp.bitwise_xor(mine, j)
        return pl.multiple_of((source * members + m) * seg, seg)

    lane = lax.broadcasted_iota(jnp.int32, (1, 128), 1)
    masks = [jnp.where(lane // HEAD_DIM == h, 1.0, 0.0).astype(BF16) for h in range(2)]
    for j in range(groups):
        for m in range(members):
            rows = pl.ds(row_of(j, m), seg)
            q = in_ref[m, 0, j]
            do = in_ref[m, 3, j]
            for h in range(2):
                q_s[h, rows, :] = q * (masks[h] * scale).astype(BF16)
                do_s[h, rows, :] = do * masks[h]
            k_s[rows, :] = in_ref[m, 1, j]
            v_s[rows, :] = in_ref[m, 2, j]
    kt_s[...] = k_s[...].T
    vt_s[...] = v_s[...].T
    dk_s[...] = jnp.zeros_like(dk_s)
    dv_s[...] = jnp.zeros_like(dv_s)
    key_index = lax.broadcasted_iota(jnp.int32, (PIECE, PIECE), 0)
    query_index = lax.broadcasted_iota(jnp.int32, (PIECE, PIECE), 1)
    causal = key_index <= query_index
    nt = (((1,), (1,)), ((), ()))

    dims = [slice(HEAD_DIM * h, HEAD_DIM * (h + 1)) for h in range(2)]
    chunk = lambda c: pl.ds(pl.multiple_of(c * PIECE, PIECE), PIECE)
    fold = lambda a, op: op(a.reshape(PIECE // 8, 8, PIECE), 0)

    def span_step(span, peaks):
        queries = chunk(span)
        q = [q_s[h, queries, :] for h in range(2)]
        do = [do_s[h, queries, :] for h in range(2)]
        q_both = jnp.concatenate(q, 0)
        do_both = jnp.concatenate(do, 0)
        piece = flag_ref[span] > 0
        tops = []
        for h in range(2):
            s = lax.dot_general(k_s[queries, :], q[h], nt, preferred_element_type=F32)
            s = jnp.where(causal | piece, s, NEG)
            s_s[h, queries, :] = s
            tops.append(fold(s, jnp.max))

        def score(c, tops):
            out = []
            for h in range(2):
                s = lax.dot_general(k_s[chunk(c), :], q[h], nt, preferred_element_type=F32)
                s_s[h, chunk(c), :] = s
                out.append(jnp.maximum(tops[h], fold(s, jnp.max)))
            return tuple(out)

        tops = lax.fori_loop(0, span, score, tuple(tops))
        tops = [jnp.max(t, 0, keepdims=True) for t in tops]

        def soften(c, sums):
            out = []
            for h in range(2):
                e = jnp.exp(s_s[h, chunk(c), :] - tops[h])
                dp = lax.dot_general(v_s[chunk(c), :], do[h], nt, preferred_element_type=F32)
                s_s[h, chunk(c), :] = e
                dp_s[h, chunk(c), :] = dp
                out.append(sums[2 * h] + fold(e, jnp.sum))
                out.append(sums[2 * h + 1] + fold(e * dp, jnp.sum))
            return tuple(out)

        sums = lax.fori_loop(0, span + 1, soften, (jnp.zeros((8, PIECE), F32),) * 4)
        sums = [jnp.sum(t, 0, keepdims=True) for t in sums]
        inverse = [1.0 / sums[0], 1.0 / sums[2]]
        delta = [sums[1] * inverse[0], sums[3] * inverse[1]]

        def combine(c, carried):
            keys = chunk(c)
            out, low_p, low_ds = [], [], []
            for h in range(2):
                p = s_s[h, keys, :] * inverse[h]
                low_p.append(p.astype(BF16))
                low_ds.append((p * (dp_s[h, keys, :] - delta[h])).astype(BF16))
                out.append(carried[2 * h] + jnp.dot(vt_s[dims[h], keys], low_p[h], preferred_element_type=F32))
                out.append(carried[2 * h + 1] + jnp.dot(kt_s[dims[h], keys], low_ds[h], preferred_element_type=F32))
            dv_s[keys, :] += jnp.dot(jnp.concatenate(low_p, 1), do_both, preferred_element_type=F32)
            dk_s[keys, :] += jnp.dot(jnp.concatenate(low_ds, 1), q_both, preferred_element_type=F32)
            return tuple(out)

        out = lax.fori_loop(0, span + 1, combine, (jnp.zeros((HEAD_DIM, PIECE), F32),) * 4)
        for h in range(2):
            ot_s[dims[h], queries] = out[2 * h]
            dqt_s[dims[h], queries] = out[2 * h + 1] * scale
        return tuple(jnp.maximum(a, b) for a, b in zip(peaks, tops))

    peaks = lax.fori_loop(0, length // PIECE, span_step, (jnp.full((1, PIECE), NEG, F32),) * 2)
    for h in range(2):
        top_ref[0, h : h + 1, :] = jnp.max(peaks[h].reshape(2, 128), 0, keepdims=True)

    back_turn = lambda u: turn_lanes(u, cos_ref[...], -low_ref[...], -high_ref[...]).astype(BF16)
    q_s[0] = ot_s[...].T.astype(BF16)
    q_s[1] = back_turn(dqt_s[...].T)
    do_s[0] = back_turn(dk_s[...])
    do_s[1] = dv_s[...].astype(BF16)
    for j in range(groups):
        for m in range(members):
            rows = pl.ds(row_of(j, m), seg)
            out_ref[m, 0, j] = q_s[0, rows, :]
            out_ref[m, 1, j] = q_s[1, rows, :]
            out_ref[m, 2, j] = do_s[0, rows, :]
            out_ref[m, 3, j] = do_s[1, rows, :]


def attend(flags, group, tables, packed):
    members, four, groups, seg, cols = packed.shape
    length = members * groups * seg
    block = pl.BlockSpec((members, four, groups, seg, 128), lambda h: (0, 0, 0, 0, h))
    table = pl.BlockSpec((length, 128), lambda h: (0, 0))
    smem = pl.BlockSpec(memory_space=pltpu.SMEM)
    tiles = (length // PIECE) * (length // PIECE + 1) // 2 * cols // HEAD_DIM
    return pl.pallas_call(
        attend_kernel,
        grid=(cols // 128,),
        in_specs=[smem, smem, table, table, table, block],
        out_specs=[block, pl.BlockSpec((1, 8, 128), lambda h: (h, 0, 0))],
        out_shape=[
            jax.ShapeDtypeStruct(packed.shape, BF16),
            jax.ShapeDtypeStruct((cols // 128, 8, 128), F32),
        ],
        scratch_shapes=[
            pltpu.VMEM((2, length, 128), BF16),
            pltpu.VMEM((length, 128), BF16),
            pltpu.VMEM((length, 128), BF16),
            pltpu.VMEM((2, length, 128), BF16),
            pltpu.VMEM((128, length), BF16),
            pltpu.VMEM((128, length), BF16),
            pltpu.VMEM((128, length), F32),
            pltpu.VMEM((128, length), F32),
            pltpu.VMEM((2, length, PIECE), F32),
            pltpu.VMEM((2, length, PIECE), F32),
            pltpu.VMEM((length, 128), F32),
            pltpu.VMEM((length, 128), F32),
        ],
        cost_estimate=pl.CostEstimate(
            flops=tiles * 5 * 2 * PIECE * PIECE * 256, bytes_accessed=packed.size * 4, transcendentals=tiles * PIECE**2
        ),
        name="attend",
    )(flags, group, *tables, packed)


def make_body(sizes):
    dp_size, group_size, pair_size = sizes["dp"], sizes["g"], sizes["m"]
    devices = dp_size * group_size * pair_size * 2
    members = pair_size * 2
    every = ("dp", "g", "m", "c")

    def swap(value, axis, k):
        return lax.ppermute(value, axis, [(i, i ^ k) for i in range(sizes[axis])])

    def butterfly(value, combine, axes):
        for axis in axes:
            k = 1
            while k < sizes[axis]:
                value = combine(value, swap(value, axis, k))
                k *= 2
        return value

    def row_at(a, i, axis=0):
        return lax.dynamic_index_in_dim(a, i, axis, keepdims=False)

    def body(
        tokens, piece_ids, cotangent, master, first_moment, second_moment, owner_slot, vectors, vector_first, vector_second
    ):
        index = {a: lax.axis_index(a) for a in every}
        group = index["g"]
        member = index["m"] * 2 + index["c"]
        me = (index["dp"] * group_size + group) * members + member
        capacity = master.shape[0]
        batch, seg = tokens.shape[0], tokens.shape[1]
        seqs = batch // group_size
        rows = batch * seg
        order = jnp.bitwise_xor(group, jnp.arange(group_size, dtype=jnp.int32))

        def leave(a):
            a = a.reshape(group_size, seqs, seg, D)
            parts = [row_at(a, group)]
            for k in range(1, group_size):
                parts.append(swap(row_at(a, jnp.bitwise_xor(group, k)), "g", k))
            return jnp.stack(parts, 1).reshape(rows, D)

        def come_home(a):
            a = a.reshape(seqs, group_size, seg, D)
            parts = [a[:, 0]] + [swap(a[:, k], "g", k) for k in range(1, group_size)]
            return jnp.take(jnp.stack(parts), order, axis=0).reshape(rows, D)

        there_tokens = leave(tokens)
        there_cotangent = leave(cotangent)
        marks = piece_ids[:, 0].reshape(group_size, seqs)
        flags = [row_at(marks, group)]
        for k in range(1, group_size):
            flags.append(swap(row_at(marks, jnp.bitwise_xor(group, k)), "g", k))
        flags = jnp.take(jnp.stack(flags), order, axis=0).T
        within = members * seg // PIECE
        flags = jnp.where(jnp.arange(within) == member * seg // PIECE, flags[:, :, None], 0)
        if within > 1:
            flags = butterfly(flags, jnp.maximum, ("c", "m"))
        flags = flags.reshape(seqs, group_size * within)

        plan = make_plan(owner_slot, devices, capacity)
        local = local_plan(plan, me)
        pers = plan["pers"]
        low_master = master.astype(BF16)
        chip_slots = jnp.concatenate([low_master, swap(low_master, "c", 1)], 0)
        held = chip_slots[local["home"]]

        def deliver(turn, held):
            send = chip_slots[local["forward_index"](turn)]
            got = lax.all_to_all(send, every, 0, 0, tiled=True)
            arrived = got[local["hole_from"]]
            return jnp.where((local["hole_round"] == turn)[:, None, None], arrived, held)

        held = deliver(0, held)
        _, held = lax.while_loop(
            lambda c: c[0] < plan["rounds"], lambda c: (c[0] + 1, deliver(c[0], c[1])), (jnp.int32(1), held)
        )
        first = lax.all_gather(held[: pers[0]], every, axis=0, tiled=True)
        first, later = lax.optimization_barrier((first, held[pers[0] :]))
        later = lax.all_gather(later, every, axis=0, tiled=True)
        from_index, to_index = plan["by_class"], []
        for per, place in zip(pers, from_index):
            dev = place // per
            other = (dev % 2 != index["c"]).astype(jnp.int32)
            to_index.append(other * (devices // 2 * per) + dev // 2 * per + place % per)

        positions = ((order[:, None] * members + member) * seg + jnp.arange(seg)[None, :]).reshape(-1)
        length = group_size * members * seg
        all_tables = rotary_lanes(jnp.arange(length, dtype=F32))
        plain = (1.0, 0.0, 0.0)
        own_tables = tuple(
            jnp.stack([t, jnp.full_like(t, c)]) for t, c in zip(rotary_lanes(positions.astype(F32)), plain)
        )
        part = group_size * seg
        group_ref = group.reshape(1).astype(jnp.int32)
        *packs, low_one = project(
            from_index[0], there_tokens, there_cotangent, vectors[0:2], first, vectors[4:7], own_tables, members, seqs
        )
        backs, tops = [], []
        for i in range(seqs):
            packed = lax.all_to_all(packs[i], ("m", "c"), 0, 0, tiled=True)
            packed = packed.reshape(members, 4, group_size, seg, D // members)
            back, top = attend(flags[i], group_ref, all_tables, packed)
            backs.append(back.reshape(members, 4, part, D // members))
            tops.append(top)
        backs, later = lax.optimization_barrier((backs, later))
        back = jnp.concatenate(backs, 2)
        back = lax.all_to_all(back, ("m", "c"), 0, 0, tiled=True)

        branch, input_part, small_mlp, keep_mlp, send_mlp = mlp(
            from_index[1], to_index[1], tokens.reshape(rows, D), cotangent.reshape(rows, D), vectors[2:4],
            vectors[8:12], vectors[12:13], later,
        )
        back, keep_mlp = lax.optimization_barrier((back, keep_mlp))
        input_one, attended, small_rest, keep_attn, send_attn = rest(
            from_index[0], to_index[0], there_tokens, there_cotangent, low_one, vectors[0:2], back, first
        )
        attended = come_home(attended)
        input_one = come_home(input_one)
        weight_out = first[from_index[0][3 * IN_MATRIX :]].reshape(D, D)
        branch_attn = jnp.dot(attended, weight_out, preferred_element_type=F32) + vectors[7]
        mixed = (branch + branch_attn).astype(BF16).reshape(tokens.shape)
        input_grad = (input_part + input_one.astype(F32)).reshape(tokens.shape)

        peaks = jnp.max(jnp.stack(tops)[:, :, :2], (0, 3)).reshape(-1)
        heads_here = HEADS // members
        peak_row = jnp.full((D,), NEG, F32)
        peak_row = lax.dynamic_update_slice(peak_row, peaks, (member * heads_here,))
        small = jnp.concatenate(
            [
                small_rest[3:5], small_mlp[4:6], small_rest[:3], small_mlp[6:7], small_mlp[:4], small_mlp[6:7], peak_row[None],
            ],
            0,
        )
        is_peak = (jnp.arange(14) == 13)[:, None]
        small = butterfly(small, lambda a, b: jnp.where(is_peak, jnp.maximum(a, b), a + b), ("c", "m", "dp", "g"))
        vector_sum, overall_peak = small[:13], small[13, :HEADS]

        def scatter_sum(value, axes):
            names = ["dp", "g", "m"]
            for axis in axes:
                at = names.index(axis)
                total = row_at(value, index[axis], at).astype(F32)
                for k in range(1, sizes[axis]):
                    sent = row_at(value, jnp.bitwise_xor(index[axis], k), at).astype(BF16)
                    got = swap(sent, axis, k)
                    total = total + got.astype(F32)
                value = total
                names.remove(axis)
            return value

        sums = []
        for k, keep, send in ((1, keep_mlp, send_mlp), (0, keep_attn, send_attn)):
            per = pers[k]
            cut = per // 2
            got = swap(send, "c", 1)
            total = keep.astype(F32) + got.astype(F32)
            total = total.reshape(dp_size, group_size, pair_size, per, BLOCK_ROWS, D)
            parts = [scatter_sum(total[..., cut:, :, :], ("dp", "m", "g"))]
            if cut:
                parts.insert(0, scatter_sum(total[..., :cut, :, :], ("m", "dp", "g")))
            sums.insert(0, jnp.concatenate(parts, 0))
        sums = jnp.concatenate(sums, 0)

        low_sums = sums.astype(BF16)

        answer, answer_round = local["answer"], local["answer_round"]

        def give_back(turn, own, other):
            got = lax.all_to_all(low_sums[local["backward_index"](turn)], every, 0, 0, tiled=True)
            here = (answer_round == turn)[:, None, None]
            own = jnp.where(here[:capacity], got[answer[:capacity]].astype(F32), own)
            other = jnp.where(here[capacity:], got[answer[capacity:]], other)
            return own, other

        own, other = give_back(0, sums[local["home_spot"][:capacity]], low_sums[local["home_spot"][capacity:]])
        _, own, other = lax.while_loop(
            lambda c: c[0] < plan["rounds"], lambda c: (c[0] + 1,) + give_back(*c), (jnp.int32(1), own, other)
        )
        from_sibling = swap(other, "c", 1).astype(F32)
        owned = jnp.where(local["holds"][:capacity, None, None], own, from_sibling)
        local_block = lax.dynamic_slice_in_dim(plan["slot_block"], me * capacity, capacity)
        holding = (local_block >= 0)[:, None, None]
        owned = jnp.where(holding, owned, 0.0)

        factors = clip_limit / jnp.maximum(overall_peak, clip_limit)
        column_scale = jnp.repeat(jnp.sqrt(factors), HEAD_DIM)
        clipped = ((local_block >= 0) & (local_block // (D // BLOCK_ROWS) < 2))[:, None, None]
        bank_new, first_new, second_new = adamw_update(master, owned, first_moment, second_moment, weight_decay)
        bank_new = jnp.where(clipped, bank_new * column_scale, bank_new)
        bank_new = jnp.where(holding, bank_new, 0.0)
        first_new = jnp.where(holding, first_new, 0.0)
        second_new = jnp.where(holding, second_new, 0.0)
        vector_new, rows_first, rows_second = adamw_update(vectors, vector_sum, vector_first, vector_second, 0.0)
        row_index = jnp.arange(13, dtype=jnp.int32)
        vector_new = jnp.where(
            ((row_index == 4) | (row_index == 5))[:, None], vector_new * column_scale, vector_new
        )
        return (
            mixed, input_grad, owned, bank_new, first_new, second_new, vector_sum, vector_new, rows_first, rows_second, factors,
        )

    return body


def solution(mesh):
    dp_size, ctx_size = mesh.shape["dp"], mesh.shape["ctx"]
    fine = Mesh(
        mesh.devices.reshape(dp_size, GROUPS, ctx_size // GROUPS // 2, 2), ("dp", "g", "m", "c")
    )
    ctx = ("g", "m", "c")
    slots = P(("dp",) + ctx, None, None)
    wide = P("dp", ctx, None)
    in_specs = (wide, P("dp", ctx), wide, slots, slots, slots, P(), P(), P(), P())
    out_specs = (wide, wide, slots, slots, slots, slots, P(), P(), P(), P(), P())
    body = make_body(dict(fine.shape))

    return jax.shard_map(body, mesh=fine, in_specs=in_specs, out_specs=out_specs, check_vma=False)
```

```python
import math

import jax
import jax.numpy as jnp
import numpy as np
from jax import lax
from jax.experimental import pallas as pl
from jax.experimental.pallas import tpu as pltpu
from jax.sharding import Mesh
from jax.sharding import PartitionSpec as P

D = 1024
HEADS = 16
HEAD_DIM = 64
FF = 4096
ROT = 16
BLOCK_ROWS = 16
PIECE = 256
GROUPS = 4
CLASSES = 2
NEG = -1e30

norm_epsilon = 1e-05
clip_limit = 4.0
beta_first = 0.9
beta_second = 0.95
learn_rate = 0.05
weight_decay = 0.1
adam_epsilon = 1e-08
adam_step = 10.0

F32 = jnp.float32
BF16 = jnp.bfloat16

CLASS_MATRICES = ((0, 1, 2, 3), (4, 5, 6, 7, 8, 9, 10, 11))


def adamw_update(weight, gradient, moment_one, moment_two, decay_rate):
    moment_one = beta_first * moment_one + (1.0 - beta_first) * gradient
    moment_two = beta_second * moment_two + (1.0 - beta_second) * gradient * gradient
    first_hat = moment_one / (1.0 - beta_first**adam_step)
    second_hat = moment_two / (1.0 - beta_second**adam_step)
    weight = weight - learn_rate * (
        first_hat / (jnp.sqrt(second_hat) + adam_epsilon) + decay_rate * weight
    )
    return (weight, moment_one, moment_two)


def norm_stats(values):
    center = values - jnp.mean(values, -1, keepdims=True)
    spread = jnp.mean(center * center, -1, keepdims=True)
    inverse = lax.rsqrt(spread + norm_epsilon)
    return center * inverse, inverse


def norm_back(grad_hat, hat, inverse):
    return inverse * (
        grad_hat
        - jnp.mean(grad_hat, -1, keepdims=True)
        - hat * jnp.mean(grad_hat * hat, -1, keepdims=True)
    )


def pick(selected, values, axes):
    return jnp.sum(jnp.where(selected, values, 0), axes)


def make_plan(owner, devices, capacity):
    blocks = owner.shape[0]
    sizes = [64 * len(c) for c in CLASS_MATRICES]
    pers = [size // devices for size in sizes]
    most = max(pers)
    per = jnp.asarray(pers, jnp.int32)
    slots = devices * capacity
    chips = devices // 2
    pair = 2 * capacity
    i32 = lambda n: jnp.arange(n, dtype=jnp.int32)
    at_slot = owner[None, :] == i32(slots)[:, None]
    slot_block = jnp.max(jnp.where(at_slot, i32(blocks)[None, :], -1), 1)
    slot_class = jnp.where(slot_block < 0, -1, jnp.where(slot_block < sizes[0], 0, 1))
    member = (slot_class[None] == i32(CLASSES)[:, None]).reshape(CLASSES, chips, pair)
    member_f = member.astype(F32)
    before = (i32(pair)[:, None] < i32(pair)[None, :]).astype(F32)
    rank = jnp.einsum("kcs,st->kct", member_f, before, preferred_element_type=F32).astype(jnp.int32)
    total = jnp.sum(member_f, -1).astype(jnp.int32)
    half = (total + 1) // 2
    second = rank >= half[..., None]
    place = rank - jnp.where(second, half[..., None], 0)
    count = jnp.stack([half, total - half], -1).reshape(CLASSES, devices)
    over = jnp.maximum(count - per[:, None], 0)
    free = jnp.maximum(per[:, None] - count, 0)
    dev = i32(devices)
    ahead = (over[:, None, :] > over[:, :, None]) | (
        (over[:, None, :] == over[:, :, None]) & (dev[None, None, :] < dev[None, :, None])
    )
    offset = jnp.sum(jnp.where(ahead, over[:, None, :], 0), -1)
    level = i32(most)
    level_start = jnp.sum(jnp.minimum(free[:, :, None], level), 1)
    valid = free[:, :, None] > level
    key = (dev[None, :] + (devices // 2) * i32(CLASSES)[:, None]) % devices
    sooner = key[:, None, :] < key[:, :, None]
    earlier = jnp.sum((sooner[..., None] & valid[:, None]).astype(jnp.int32), 2)
    order = level_start[:, None, :] + earlier
    owns = (
        (order[..., None] >= offset[:, None, None, :])
        & (order[..., None] < (offset + over)[:, None, None, :])
        & valid[..., None]
    )
    source = pick(owns, dev, -1)
    flat = lambda a: a.transpose(1, 0, 2).reshape(devices, CLASSES * most)
    source_f, valid_f = flat(source), flat(valid)
    extra_f = flat(order - pick(owns, offset[:, None, None, :], -1))
    index_f = i32(CLASSES * most)
    same = (
        (source_f[:, :, None] // 2 == source_f[:, None, :] // 2)
        & valid_f[:, None, :]
        & (index_f[None, :] < index_f[:, None])
    )
    turn_f = jnp.sum(same.astype(jnp.int32), -1)
    rounds = jnp.max(jnp.where(valid_f, turn_f // 2 + 1, 0))
    turn = turn_f.reshape(devices, CLASSES, most).transpose(1, 0, 2)
    home_dev = 2 * i32(chips)[None, :, None] + second
    halves = offset.reshape(CLASSES, chips, 2)
    offset_s = jnp.where(second, halves[..., 1:], halves[..., :1])
    per_s = per[:, None, None]
    wanted = (offset_s + place - per_s).reshape(CLASSES, slots)
    hole_position = dev[None, :, None] * per_s + count[..., None] + level
    filled = jnp.where(valid, order, -1).reshape(CLASSES, devices * most)
    moved = pick(
        wanted[:, :, None] == filled[:, None, :],
        hole_position.reshape(CLASSES, 1, devices * most),
        -1,
    )
    position = jnp.where(place < per_s, home_dev * per_s + place, moved.reshape(CLASSES, chips, pair))
    position = jnp.sum(jnp.where(member, position, 0), 0).reshape(slots)
    block_position = pick(at_slot, position[:, None], 0)
    by_class, at_position, first = [], [], 0
    for size in sizes:
        mine = block_position[first : first + size]
        by_class.append(mine)
        at_position.append(pick(mine[:, None] == i32(size)[None, :], i32(size)[:, None], 0))
        first += size
    return dict(
        pers=pers, per=per, most=most, slot_block=slot_block, member=member, second=second, place=place, count=count,
        offset=offset, order=order, valid=valid, turn=turn, source_f=source_f, valid_f=valid_f, extra_f=extra_f,
        turn_f=turn_f, rounds=rounds, by_class=by_class, at_position=at_position, pair=pair, capacity=capacity,
        devices=devices,
    )


def local_plan(plan, me):
    pers, most, pair, capacity, devices = (plan[n] for n in ("pers", "most", "pair", "capacity", "devices"))
    per = plan["per"][:, None]
    row = lambda a, i, axis: lax.dynamic_index_in_dim(a, i, axis, keepdims=False)
    i32 = lambda n: jnp.arange(n, dtype=jnp.int32)
    chip, mine = me // 2, me % 2
    member, second, place = (row(plan[n], chip, 1) for n in ("member", "second", "place"))
    held = member & (second.astype(jnp.int32) == mine)
    slot = i32(pair)
    where_slot = jnp.where(slot // capacity == mine, slot % capacity, capacity + slot % capacity)
    spot = i32(most)
    home = pick(held[:, None, :] & (place[:, None, :] == spot[None, :, None]), where_slot, -1)
    count = row(plan["count"], me, 1)
    hole = spot[None, :, None] - count[:, None, None] == spot[None, None, :]
    valid_me, turn_me = row(plan["valid"], me, 1), row(plan["turn"], me, 1)
    source_me = row(plan["source_f"], me, 0).reshape(CLASSES, most)
    hole_from = pick(hole, (source_me // 2 * 2 + turn_me % 2)[:, None, :], -1)
    hole_round = jnp.sum(jnp.where(hole & valid_me[:, None, :], turn_me[:, None, :] // 2 + 1, 0), -1) - 1
    flat = lambda a: jnp.concatenate([a[k, :p] for k, p in enumerate(pers)])
    sent = plan["valid_f"] & (plan["source_f"] // 2 == chip) & (plan["turn_f"] % 2 == mine)
    class_f = jnp.repeat(i32(CLASSES), most)
    beyond_slot = jnp.where(member, 2 * (place - per) + second, -1)

    def forward_index(turn):
        here = sent & (plan["turn_f"] // 2 == turn)
        kind = jnp.where(jnp.any(here, -1), pick(here, class_f, -1), CLASSES)
        beyond = pick(here, 2 * plan["extra_f"] + plan["source_f"] % 2, -1)
        match = (kind[:, None, None] == i32(CLASSES)[None, :, None]) & (beyond_slot[None] == beyond[:, None, None])
        return pick(match, where_slot, (1, 2))

    first = np.cumsum([0] + pers[:-1]).astype(np.int32)[:, None]
    spot_f = (first + count[:, None] + spot[None, :]).reshape(-1)
    back_to = jnp.where(valid_me, source_me // 2 * 2 + turn_me % 2, -1).reshape(-1)
    back_round = (turn_me // 2).reshape(-1)

    def backward_index(turn):
        match = (back_to[None, :] == i32(devices)[:, None]) & (back_round == turn)[None, :]
        return pick(match, spot_f, -1)

    beyond = member & (place >= per)
    offsets = row(plan["offset"].reshape(CLASSES, devices // 2, 2), chip, 1)
    want = jnp.where(beyond, jnp.where(second, offsets[:, 1:], offsets[:, :1]) + place - per, -1)
    filled = jnp.where(plan["valid"], plan["order"], -2).reshape(CLASSES, 1, -1)
    match = want[:, :, None] == filled
    code = plan["turn"] * devices + i32(devices)[None, :, None]
    code = pick(match, code.reshape(CLASSES, 1, -1), (0, 2))
    beyond = jnp.any(beyond, 0)
    answer = code % devices
    answer_turn = code // devices
    answer_round = jnp.where(beyond & (answer_turn % 2 == mine), answer_turn // 2, -1)
    home_spot = pick(member & (place < per), first + place, 0)
    holds = jnp.where(beyond, answer_turn % 2 == mine, jnp.any(held, 0))
    sort_pair = lambda a: jnp.where(mine == 0, a, jnp.concatenate([a[capacity:], a[:capacity]]))
    return dict(
        home=flat(home), hole_from=flat(hole_from), hole_round=flat(hole_round), forward_index=forward_index,
        backward_index=backward_index, answer=sort_pair(answer), answer_round=sort_pair(answer_round),
        home_spot=sort_pair(home_spot), holds=sort_pair(holds),
    )


def rotary_lanes(positions):
    halves = jnp.arange(ROT // 2, dtype=F32)
    inverse = jnp.exp(-math.log(10000.0) * 2.0 * halves / ROT)
    angles = positions[:, None] * inverse[None, :]
    cos, sin = jnp.cos(angles), jnp.sin(angles)
    rest = HEAD_DIM - ROT
    ones, zeros = jnp.ones((positions.shape[0], rest), F32), jnp.zeros((positions.shape[0], rest), F32)
    blank = jnp.zeros_like(sin)
    cos_row = jnp.concatenate([cos, cos, ones], -1)
    low_row = jnp.concatenate([-sin, blank, zeros], -1)
    high_row = jnp.concatenate([blank, sin, zeros], -1)
    return tuple(jnp.concatenate([t, t], -1) for t in (cos_row, low_row, high_row))


def turn_lanes(u, cos, low, high):
    width = u.shape[-1]
    return u * cos + pltpu.roll(u, width - ROT // 2, 1) * low + pltpu.roll(u, ROT // 2, 1) * high


def fetch_blocks(index_ref, first, count, blocks_ref, matrix_ref, sem):
    @pl.loop(0, count)
    def _(i):
        rows = pl.ds(pl.multiple_of(i * BLOCK_ROWS, BLOCK_ROWS), BLOCK_ROWS)
        pltpu.make_async_copy(blocks_ref.at[index_ref[first + i]], matrix_ref.at[rows], sem).start()


def wait_blocks(matrix_ref, sem):
    pltpu.make_async_copy(matrix_ref, matrix_ref, sem).wait()


def store_blocks(index_ref, first, count, matrix_ref, keep_ref, send_ref, sem):
    half = keep_ref.shape[0]

    @pl.loop(0, count)
    def _(i):
        rows = pl.ds(pl.multiple_of(i * BLOCK_ROWS, BLOCK_ROWS), BLOCK_ROWS)
        to = index_ref[first + i]

        @pl.when(to < half)
        def _():
            pltpu.make_async_copy(matrix_ref.at[rows], keep_ref.at[to], sem).start()

        @pl.when(to >= half)
        def _():
            pltpu.make_async_copy(matrix_ref.at[rows], send_ref.at[to - half], sem).start()


IN_MATRIX = D // BLOCK_ROWS
NT = (((1,), (1,)), ((), ()))
TILE = 256
WIDE = 384


def project_kernel(index_ref, x_ref, e_ref, gain_ref, b_ref, cos_ref, low_ref, high_ref, blocks_ref, *refs):
    *out_refs, h_ref, w_s, sems = refs
    kind = pl.program_id(0)
    slot = kind % 2
    part = out_refs[0].shape[2]
    members, cols = out_refs[0].shape[0], out_refs[0].shape[3]

    @pl.when(kind == 0)
    def _():
        fetch_blocks(index_ref, 0, IN_MATRIX, blocks_ref, w_s.at[0], sems.at[0])
        for i in range(len(out_refs)):
            rows = slice(part * i, part * (i + 1))
            hat, _ = norm_stats(x_ref[rows, :].astype(F32))
            h_ref[rows, :] = (hat * gain_ref[0:1, :] + gain_ref[1:2, :]).astype(BF16)

    wait_blocks(w_s.at[slot], sems.at[slot])

    @pl.when(kind < 3)
    def _():
        fetch_blocks(index_ref, (kind + 1) * IN_MATRIX, IN_MATRIX, blocks_ref, w_s.at[1 - slot], sems.at[1 - slot])

    for m in range(members):
        lanes = slice(cols * m, cols * (m + 1))

        @pl.when(kind < 3)
        def _(lanes=lanes, m=m):
            u = jnp.dot(h_ref[...], w_s[slot, :, lanes], preferred_element_type=F32) + b_ref[0, :, lanes]
            for i, out_ref in enumerate(out_refs):
                rows = slice(part * i, part * (i + 1))
                turned = [
                    turn_lanes(u[rows, 128 * j : 128 * (j + 1)], cos_ref[0], low_ref[0], high_ref[0])
                    for j in range(cols // 128)
                ]
                out_ref[m, 0] = jnp.concatenate(turned, 1).astype(BF16)

        @pl.when(kind == 3)
        def _(lanes=lanes, m=m):
            u = lax.dot_general(e_ref[...], w_s[slot, lanes, :], NT, preferred_element_type=F32).astype(BF16)
            for i, out_ref in enumerate(out_refs):
                out_ref[m, 0] = u[part * i : part * (i + 1)]


def project(index, x, e, gains, blocks, biases, tables, members, seqs):
    rows = x.shape[0]
    part = rows // seqs
    cols = D // members
    whole = lambda shape: pl.BlockSpec(shape, lambda k: (0,) * len(shape))
    once = lambda shape: pl.BlockSpec(shape, lambda k: (0,) * len(shape), pipeline_mode=pl.Buffered(1))
    table = pl.BlockSpec((1, part, 128), lambda k: (jnp.where(k < 2, 0, 1), 0, 0))
    return pl.pallas_call(
        project_kernel,
        grid=(4,),
        in_specs=[
            pl.BlockSpec(memory_space=pltpu.SMEM),
            once((rows, D)),
            once((rows, D)),
            whole((2, D)),
            pl.BlockSpec((1, 1, D), lambda k: (jnp.minimum(k, 2), 0, 0)),
            table,
            table,
            table,
            pl.BlockSpec(memory_space=pl.ANY),
        ],
        out_specs=[pl.BlockSpec((members, 1, part, cols), lambda k: (0, k, 0, 0))] * seqs + [whole((rows, D))],
        out_shape=[jax.ShapeDtypeStruct((members, 4, part, cols), BF16)] * seqs
        + [jax.ShapeDtypeStruct((rows, D), BF16)],
        scratch_shapes=[pltpu.VMEM((2, D, D), BF16), pltpu.SemaphoreType.DMA((2,))],
        cost_estimate=pl.CostEstimate(
            flops=2 * rows * D * 4 * D, bytes_accessed=8 * D * D + 14 * rows * D, transcendentals=0
        ),
        name="project",
    )(index, x, e, gains, biases.reshape(3, 1, D), *tables, blocks)


def mlp_kernel(
    index_ref, to_ref, x_ref, e_ref, gain_ref, b_ref, last_ref, blocks_ref,
    mixed_ref, input_ref, small_ref, keep_ref, send_ref,
    h_s, ht_s, up_s, down_s, act_s, pre_s, at_s, back_s, stage_u, stage_d, in_sems, out_sems,
):
    step, steps = pl.program_id(0), pl.num_programs(0)
    slot = step % 2
    rows_all = x_ref.shape[0]
    tiles = rows_all // TILE

    def fetch(j, slot):
        fetch_blocks(index_ref, j * IN_MATRIX, IN_MATRIX, blocks_ref, up_s.at[slot], in_sems.at[slot])
        fetch_blocks(index_ref, (steps + j) * IN_MATRIX, IN_MATRIX, blocks_ref, down_s.at[slot], in_sems.at[2 + slot])

    @pl.when(step == 0)
    def _():
        fetch(0, 0)

        @pl.loop(0, tiles)
        def _(t):
            rows = pl.ds(pl.multiple_of(t * TILE, TILE), TILE)
            x = x_ref[rows, :].astype(F32)
            hat, _ = norm_stats(x)
            h_s[rows, :] = (hat * gain_ref[0:1, :] + gain_ref[1:2, :]).astype(BF16)
            mixed_ref[rows, :] = x + last_ref[...]
            back_s[rows, :] = jnp.zeros((TILE, D), F32)

        ht_s[...] = h_s[...].T
        small_ref[...] = jnp.zeros_like(small_ref)

    wait_blocks(up_s.at[slot], in_sems.at[slot])
    wait_blocks(down_s.at[slot], in_sems.at[2 + slot])

    @pl.when(step + 1 < steps)
    def _():
        fetch(step + 1, 1 - slot)

    up, down = up_s.at[slot], down_s.at[slot]

    @pl.loop(0, rows_all // WIDE)
    def _(t):
        rows = pl.ds(pl.multiple_of(t * WIDE, WIDE), WIDE)
        h, e = h_s[rows, :], e_ref[rows, :]
        for c in range(D // TILE):
            lanes = slice(TILE * c, TILE * (c + 1))
            before = jnp.dot(h, up[:, lanes], preferred_element_type=F32) + b_ref[0, :, lanes]
            grad = lax.dot_general(e, down[lanes, :], NT, preferred_element_type=F32)
            cdf = 0.5 * (1.0 + lax.erf(before * (0.5**0.5)))
            act_s[rows, lanes] = (before * cdf).astype(BF16)
            slope = cdf + before * jnp.exp(-0.5 * before * before) * ((2.0 * math.pi) ** -0.5)
            pre = (grad * slope).astype(BF16)
            pre_s[rows, lanes] = pre
            total = jnp.sum(pre.astype(F32), 0, keepdims=True)
            small_ref[pl.ds(step, 1), lanes] += total

    @pl.when(step > 0)
    def _():
        wait_blocks(stage_u, out_sems.at[0])
        wait_blocks(stage_d, out_sems.at[1])

    at_s[...] = act_s[...].T
    for c in range(D // TILE):
        lanes = slice(TILE * c, TILE * (c + 1))
        stage_u[:, lanes] = jnp.dot(ht_s[...], pre_s[:, lanes], preferred_element_type=F32).astype(BF16)
    store_blocks(to_ref, step * IN_MATRIX, IN_MATRIX, stage_u, keep_ref, send_ref, out_sems.at[0])
    for c in range(D // TILE):
        lanes = slice(TILE * c, TILE * (c + 1))
        stage_d[:, lanes] = jnp.dot(at_s[...], e_ref[:, lanes], preferred_element_type=F32).astype(BF16)
    store_blocks(to_ref, (steps + step) * IN_MATRIX, IN_MATRIX, stage_d, keep_ref, send_ref, out_sems.at[1])
    for c in range(D // TILE):
        lanes = slice(TILE * c, TILE * (c + 1))
        mixed_ref[:, lanes] += jnp.dot(act_s[...], down[:, lanes], preferred_element_type=F32)
        back_s[:, lanes] += lax.dot_general(pre_s[...], up[lanes, :], NT, preferred_element_type=F32)

    @pl.when(step == steps - 1)
    def _():
        @pl.loop(0, tiles)
        def _(t):
            rows = pl.ds(pl.multiple_of(t * TILE, TILE), TILE)
            hat, inverse = norm_stats(x_ref[rows, :].astype(F32))
            back = back_s[rows, :]
            e = e_ref[rows, :].astype(F32)
            input_ref[rows, :] = e + norm_back(back * gain_ref[0:1, :], hat, inverse)
            small_ref[4:5, :] += jnp.sum(back * hat, 0, keepdims=True)
            small_ref[5:6, :] += jnp.sum(back, 0, keepdims=True)
            small_ref[6:7, :] += jnp.sum(e, 0, keepdims=True)

        wait_blocks(stage_u, out_sems.at[0])
        wait_blocks(stage_d, out_sems.at[1])


def mlp(index, to, x, e, gains, biases, last, blocks):
    rows = x.shape[0]
    steps = biases.shape[0]
    half = blocks.shape[0] // 2
    whole = lambda shape: pl.BlockSpec(shape, lambda k: (0,) * len(shape), pipeline_mode=pl.Buffered(1))
    smem = pl.BlockSpec(memory_space=pltpu.SMEM)
    hbm = pl.BlockSpec(memory_space=pl.ANY)
    halves = jax.ShapeDtypeStruct((half, BLOCK_ROWS, D), BF16)
    return pl.pallas_call(
        mlp_kernel,
        grid=(steps,),
        in_specs=[
            smem, smem, whole((rows, D)), whole((rows, D)), whole((2, D)),
            pl.BlockSpec((1, 1, D), lambda k: (k, 0, 0)), whole((1, D)), hbm,
        ],
        out_specs=[
            pl.BlockSpec((rows, D), lambda k: (0, 0)),
            pl.BlockSpec((rows, D), lambda k: (0, 0)),
            pl.BlockSpec((8, D), lambda k: (0, 0)),
            hbm,
            hbm,
        ],
        out_shape=[
            jax.ShapeDtypeStruct((rows, D), F32), jax.ShapeDtypeStruct((rows, D), F32),
            jax.ShapeDtypeStruct((8, D), F32), halves, halves,
        ],
        scratch_shapes=[
            pltpu.VMEM((rows, D), BF16),
            pltpu.VMEM((D, rows), BF16),
            pltpu.VMEM((2, D, D), BF16),
            pltpu.VMEM((2, D, D), BF16),
            pltpu.VMEM((rows, D), BF16),
            pltpu.VMEM((rows, D), BF16),
            pltpu.VMEM((D, rows), BF16),
            pltpu.VMEM((rows, D), F32),
            pltpu.VMEM((D, D), BF16),
            pltpu.VMEM((D, D), BF16),
            pltpu.SemaphoreType.DMA((4,)),
            pltpu.SemaphoreType.DMA((2,)),
        ],
        cost_estimate=pl.CostEstimate(
            flops=12 * rows * D * FF, bytes_accessed=8 * D * FF + 12 * rows * D, transcendentals=2 * rows * FF
        ),
        name="mlp",
    )(index, to, x, e, gains, biases.reshape(steps, 1, D), last, blocks)


def rest_kernel(
    index_ref, to_ref, x_ref, e_ref, h_ref, gain_ref, head_ref, tail_ref, blocks_ref,
    input_ref, o_ref, small_ref, keep_ref, send_ref,
    ht_s, w_s, grad_s, sum_s, stage_s, in_sems, out_sems,
):
    step = pl.program_id(0)
    slot = step % 2
    members, _, part, cols = head_ref.shape
    tiles = x_ref.shape[0] // TILE

    @pl.when(step == 0)
    def _():
        fetch_blocks(index_ref, 0, IN_MATRIX, blocks_ref, w_s.at[0], in_sems.at[0])
        ht_s[...] = h_ref[...].T
        sum_s[...] = jnp.zeros_like(sum_s)
        small_ref[...] = jnp.zeros_like(small_ref)

    @pl.when(step < 2)
    def _():
        fetch_blocks(index_ref, (step + 1) * IN_MATRIX, IN_MATRIX, blocks_ref, w_s.at[1 - slot], in_sems.at[1 - slot])

    for m in range(members):
        grad_s[:part, cols * m : cols * (m + 1)] = head_ref[m, 0]
        grad_s[part:, cols * m : cols * (m + 1)] = tail_ref[m, 0]

    @pl.when(step > 1)
    def _():
        wait_blocks(stage_s.at[slot], out_sems.at[slot])

    @pl.when(step < 3)
    def _():
        wait_blocks(w_s.at[slot], in_sems.at[slot])

        for c in range(D // TILE):
            lanes = slice(TILE * c, TILE * (c + 1))
            stage_s[slot, :, lanes] = jnp.dot(
                ht_s[...], grad_s[:, lanes], preferred_element_type=F32
            ).astype(BF16)
            sum_s[:, lanes] += lax.dot_general(grad_s[...], w_s[slot, lanes, :], NT, preferred_element_type=F32)

        @pl.loop(0, tiles)
        def _(t):
            rows = pl.ds(pl.multiple_of(t * TILE, TILE), TILE)
            small_ref[pl.ds(step, 1), :] += jnp.sum(grad_s[rows, :].astype(F32), 0, keepdims=True)

    @pl.when(step == 3)
    def _():
        o_ref[...] = grad_s[...]
        ht_s[...] = grad_s[...].T
        for c in range(D // TILE):
            lanes = slice(TILE * c, TILE * (c + 1))
            stage_s[slot, :, lanes] = jnp.dot(
                ht_s[...], e_ref[:, lanes], preferred_element_type=F32
            ).astype(BF16)

    store_blocks(to_ref, step * IN_MATRIX, IN_MATRIX, stage_s.at[slot], keep_ref, send_ref, out_sems.at[slot])

    @pl.when(step == 3)
    def _():
        @pl.loop(0, tiles)
        def _(t):
            rows = pl.ds(pl.multiple_of(t * TILE, TILE), TILE)
            hat, inverse = norm_stats(x_ref[rows, :].astype(F32))
            grad = sum_s[rows, :]
            input_ref[rows, :] = norm_back(grad * gain_ref[0:1, :], hat, inverse).astype(BF16)
            small_ref[3:4, :] += jnp.sum(grad * hat, 0, keepdims=True)
            small_ref[4:5, :] += jnp.sum(grad, 0, keepdims=True)

        wait_blocks(stage_s.at[0], out_sems.at[0])
        wait_blocks(stage_s.at[1], out_sems.at[1])


def rest(index, to, x, e, h, gains, head, tail, blocks):
    rows = x.shape[0]
    members, _, part, cols = head.shape
    half = blocks.shape[0] // 2
    once = lambda shape: pl.BlockSpec(shape, lambda k: (0,) * len(shape), pipeline_mode=pl.Buffered(1))
    whole = lambda shape: pl.BlockSpec(shape, lambda k: (0,) * len(shape))
    smem = pl.BlockSpec(memory_space=pltpu.SMEM)
    hbm = pl.BlockSpec(memory_space=pl.ANY)
    halves = jax.ShapeDtypeStruct((half, BLOCK_ROWS, D), BF16)
    return pl.pallas_call(
        rest_kernel,
        grid=(4,),
        in_specs=[
            smem, smem, once((rows, D)), once((rows, D)), once((rows, D)), once((2, D)),
            pl.BlockSpec((members, 1, part, cols), lambda k: (0, (k + 1) % 4, 0, 0)),
            pl.BlockSpec((members, 1, rows - part, cols), lambda k: (0, (k + 1) % 4, 0, 0)), hbm,
        ],
        out_specs=[whole((rows, D)), whole((rows, D)), whole((8, D)), hbm, hbm],
        out_shape=[
            jax.ShapeDtypeStruct((rows, D), BF16), jax.ShapeDtypeStruct((rows, D), BF16),
            jax.ShapeDtypeStruct((8, D), F32), halves, halves,
        ],
        scratch_shapes=[
            pltpu.VMEM((D, rows), BF16),
            pltpu.VMEM((2, D, D), BF16),
            pltpu.VMEM((rows, D), BF16),
            pltpu.VMEM((rows, D), F32),
            pltpu.VMEM((2, D, D), BF16),
            pltpu.SemaphoreType.DMA((2,)),
            pltpu.SemaphoreType.DMA((2,)),
        ],
        cost_estimate=pl.CostEstimate(
            flops=14 * rows * D * D, bytes_accessed=14 * D * D + 20 * rows * D, transcendentals=0
        ),
        name="rest",
    )(index, to, x, e, h, gains, head, tail, blocks)


def attend_kernel(
    flag_ref, mine_ref, cos_ref, low_ref, high_ref, in_ref, out_ref, top_ref,
    q_s, k_s, v_s, do_s, kt_s, vt_s, ot_s, dqt_s, s_s, dp_s, dk_s, dv_s,
):
    members, _, groups, seg, _ = in_ref.shape
    length = members * groups * seg
    mine = mine_ref[0]
    scale = HEAD_DIM**-0.5

    def row_of(j, m):
        source = jnp.bitwise_xor(mine, j)
        return pl.multiple_of((source * members + m) * seg, seg)

    lane = lax.broadcasted_iota(jnp.int32, (1, 128), 1)
    masks = [jnp.where(lane // HEAD_DIM == h, 1.0, 0.0).astype(BF16) for h in range(2)]
    for j in range(groups):
        for m in range(members):
            rows = pl.ds(row_of(j, m), seg)
            q = in_ref[m, 0, j]
            do = in_ref[m, 3, j]
            for h in range(2):
                q_s[h, rows, :] = q * (masks[h] * scale).astype(BF16)
                do_s[h, rows, :] = do * masks[h]
            k_s[rows, :] = in_ref[m, 1, j]
            v_s[rows, :] = in_ref[m, 2, j]
    kt_s[...] = k_s[...].T
    vt_s[...] = v_s[...].T
    dk_s[...] = jnp.zeros_like(dk_s)
    dv_s[...] = jnp.zeros_like(dv_s)
    key_index = lax.broadcasted_iota(jnp.int32, (PIECE, PIECE), 0)
    query_index = lax.broadcasted_iota(jnp.int32, (PIECE, PIECE), 1)
    causal = key_index <= query_index
    nt = (((1,), (1,)), ((), ()))

    dims = [slice(HEAD_DIM * h, HEAD_DIM * (h + 1)) for h in range(2)]
    chunk = lambda c: pl.ds(pl.multiple_of(c * PIECE, PIECE), PIECE)
    fold = lambda a, op: op(a.reshape(PIECE // 8, 8, PIECE), 0)

    def span_step(span, peaks):
        queries = chunk(span)
        q = [q_s[h, queries, :] for h in range(2)]
        do = [do_s[h, queries, :] for h in range(2)]
        q_both = jnp.concatenate(q, 0)
        do_both = jnp.concatenate(do, 0)
        piece = flag_ref[span] > 0
        tops = []
        for h in range(2):
            s = lax.dot_general(k_s[queries, :], q[h], nt, preferred_element_type=F32)
            s = jnp.where(causal | piece, s, NEG)
            s_s[h, queries, :] = s
            tops.append(fold(s, jnp.max))

        def score(c, tops):
            out = []
            for h in range(2):
                s = lax.dot_general(k_s[chunk(c), :], q[h], nt, preferred_element_type=F32)
                s_s[h, chunk(c), :] = s
                out.append(jnp.maximum(tops[h], fold(s, jnp.max)))
            return tuple(out)

        tops = lax.fori_loop(0, span, score, tuple(tops))
        tops = [jnp.max(t, 0, keepdims=True) for t in tops]

        def soften(c, sums):
            out = []
            for h in range(2):
                e = jnp.exp(s_s[h, chunk(c), :] - tops[h])
                dp = lax.dot_general(v_s[chunk(c), :], do[h], nt, preferred_element_type=F32)
                s_s[h, chunk(c), :] = e
                dp_s[h, chunk(c), :] = dp
                out.append(sums[2 * h] + fold(e, jnp.sum))
                out.append(sums[2 * h + 1] + fold(e * dp, jnp.sum))
            return tuple(out)

        sums = lax.fori_loop(0, span + 1, soften, (jnp.zeros((8, PIECE), F32),) * 4)
        sums = [jnp.sum(t, 0, keepdims=True) for t in sums]
        inverse = [1.0 / sums[0], 1.0 / sums[2]]
        delta = [sums[1] * inverse[0], sums[3] * inverse[1]]

        def combine(c, carried):
            keys = chunk(c)
            out, low_p, low_ds = [], [], []
            for h in range(2):
                p = s_s[h, keys, :] * inverse[h]
                low_p.append(p.astype(BF16))
                low_ds.append((p * (dp_s[h, keys, :] - delta[h])).astype(BF16))
                out.append(carried[2 * h] + jnp.dot(vt_s[dims[h], keys], low_p[h], preferred_element_type=F32))
                out.append(carried[2 * h + 1] + jnp.dot(kt_s[dims[h], keys], low_ds[h], preferred_element_type=F32))
            dv_s[keys, :] += jnp.dot(jnp.concatenate(low_p, 1), do_both, preferred_element_type=F32)
            dk_s[keys, :] += jnp.dot(jnp.concatenate(low_ds, 1), q_both, preferred_element_type=F32)
            return tuple(out)

        out = lax.fori_loop(0, span + 1, combine, (jnp.zeros((HEAD_DIM, PIECE), F32),) * 4)
        for h in range(2):
            ot_s[dims[h], queries] = out[2 * h]
            dqt_s[dims[h], queries] = out[2 * h + 1] * scale
        return tuple(jnp.maximum(a, b) for a, b in zip(peaks, tops))

    peaks = lax.fori_loop(0, length // PIECE, span_step, (jnp.full((1, PIECE), NEG, F32),) * 2)
    for h in range(2):
        top_ref[0, h : h + 1, :] = jnp.max(peaks[h].reshape(2, 128), 0, keepdims=True)

    back_turn = lambda u: turn_lanes(u, cos_ref[...], -low_ref[...], -high_ref[...]).astype(BF16)
    q_s[0] = ot_s[...].T.astype(BF16)
    q_s[1] = back_turn(dqt_s[...].T)
    do_s[0] = back_turn(dk_s[...])
    do_s[1] = dv_s[...].astype(BF16)
    for j in range(groups):
        for m in range(members):
            rows = pl.ds(row_of(j, m), seg)
            out_ref[m, 0, j] = q_s[0, rows, :]
            out_ref[m, 1, j] = q_s[1, rows, :]
            out_ref[m, 2, j] = do_s[0, rows, :]
            out_ref[m, 3, j] = do_s[1, rows, :]


def attend(flags, group, tables, packed):
    members, four, groups, seg, cols = packed.shape
    length = members * groups * seg
    block = pl.BlockSpec((members, four, groups, seg, 128), lambda h: (0, 0, 0, 0, h))
    table = pl.BlockSpec((length, 128), lambda h: (0, 0))
    smem = pl.BlockSpec(memory_space=pltpu.SMEM)
    tiles = (length // PIECE) * (length // PIECE + 1) // 2 * cols // HEAD_DIM
    return pl.pallas_call(
        attend_kernel,
        grid=(cols // 128,),
        in_specs=[smem, smem, table, table, table, block],
        out_specs=[block, pl.BlockSpec((1, 8, 128), lambda h: (h, 0, 0))],
        out_shape=[
            jax.ShapeDtypeStruct(packed.shape, BF16),
            jax.ShapeDtypeStruct((cols // 128, 8, 128), F32),
        ],
        scratch_shapes=[
            pltpu.VMEM((2, length, 128), BF16),
            pltpu.VMEM((length, 128), BF16),
            pltpu.VMEM((length, 128), BF16),
            pltpu.VMEM((2, length, 128), BF16),
            pltpu.VMEM((128, length), BF16),
            pltpu.VMEM((128, length), BF16),
            pltpu.VMEM((128, length), F32),
            pltpu.VMEM((128, length), F32),
            pltpu.VMEM((2, length, PIECE), F32),
            pltpu.VMEM((2, length, PIECE), F32),
            pltpu.VMEM((length, 128), F32),
            pltpu.VMEM((length, 128), F32),
        ],
        cost_estimate=pl.CostEstimate(
            flops=tiles * 5 * 2 * PIECE * PIECE * 256, bytes_accessed=packed.size * 4, transcendentals=tiles * PIECE**2
        ),
        name="attend",
    )(flags, group, *tables, packed)


def make_body(sizes):
    dp_size, group_size, pair_size = sizes["dp"], sizes["g"], sizes["m"]
    devices = dp_size * group_size * pair_size * 2
    members = pair_size * 2
    every = ("dp", "g", "m", "c")

    def swap(value, axis, k):
        return lax.ppermute(value, axis, [(i, i ^ k) for i in range(sizes[axis])])

    def butterfly(value, combine, axes):
        for axis in axes:
            k = 1
            while k < sizes[axis]:
                value = combine(value, swap(value, axis, k))
                k *= 2
        return value

    def row_at(a, i, axis=0):
        return lax.dynamic_index_in_dim(a, i, axis, keepdims=False)

    def body(
        tokens, piece_ids, cotangent, master, first_moment, second_moment, owner_slot, vectors, vector_first, vector_second
    ):
        index = {a: lax.axis_index(a) for a in every}
        group = index["g"]
        member = index["m"] * 2 + index["c"]
        me = (index["dp"] * group_size + group) * members + member
        capacity = master.shape[0]
        batch, seg = tokens.shape[0], tokens.shape[1]
        seqs = batch // group_size
        rows = batch * seg
        order = jnp.bitwise_xor(group, jnp.arange(group_size, dtype=jnp.int32))

        def leave(a):
            a = a.reshape(group_size, seqs, seg, D)
            parts = [row_at(a, group)]
            for k in range(1, group_size):
                parts.append(swap(row_at(a, jnp.bitwise_xor(group, k)), "g", k))
            return jnp.stack(parts, 1).reshape(rows, D)

        def come_home(a):
            a = a.reshape(seqs, group_size, seg, D)
            parts = [a[:, 0]] + [swap(a[:, k], "g", k) for k in range(1, group_size)]
            parts = jnp.stack(parts)
            return jnp.take(parts, order, axis=0).reshape(rows, D)

        there_tokens = leave(tokens)
        there_cotangent = leave(cotangent)
        marks = piece_ids[:, 0].reshape(group_size, seqs)
        flags = [row_at(marks, group)]
        for k in range(1, group_size):
            flags.append(swap(row_at(marks, jnp.bitwise_xor(group, k)), "g", k))
        flags = jnp.take(jnp.stack(flags), order, axis=0).T
        within = members * seg // PIECE
        flags = jnp.where(jnp.arange(within) == member * seg // PIECE, flags[:, :, None], 0)
        if within > 1:
            flags = butterfly(flags, jnp.maximum, ("c", "m"))
        flags = flags.reshape(seqs, group_size * within)

        plan = make_plan(owner_slot, devices, capacity)
        local = local_plan(plan, me)
        pers = plan["pers"]
        low_master = master.astype(BF16)
        chip_slots = jnp.concatenate([low_master, swap(low_master, "c", 1)], 0)
        held = chip_slots[local["home"]]

        def deliver(turn, held):
            send = chip_slots[local["forward_index"](turn)]
            got = lax.all_to_all(send, every, 0, 0, tiled=True)
            arrived = got[local["hole_from"]]
            return jnp.where((local["hole_round"] == turn)[:, None, None], arrived, held)

        held = deliver(0, held)
        _, held = lax.while_loop(
            lambda c: c[0] < plan["rounds"], lambda c: (c[0] + 1, deliver(c[0], c[1])), (jnp.int32(1), held)
        )
        first = lax.all_gather(held[: pers[0]], every, axis=0, tiled=True)
        first, later = lax.optimization_barrier((first, held[pers[0] :]))
        later = lax.all_gather(later, every, axis=0, tiled=True)
        from_index, to_index = plan["by_class"], []
        for per, place in zip(pers, from_index):
            dev = place // per
            other = (dev % 2 != index["c"]).astype(jnp.int32)
            to_index.append(other * (devices // 2 * per) + dev // 2 * per + place % per)

        positions = ((order[:, None] * members + member) * seg + jnp.arange(seg)[None, :]).reshape(-1)
        length = group_size * members * seg
        all_tables = rotary_lanes(jnp.arange(length, dtype=F32))
        plain = (1.0, 0.0, 0.0)
        own_tables = tuple(
            jnp.stack([t, jnp.full_like(t, c)]) for t, c in zip(rotary_lanes(positions.astype(F32)), plain)
        )
        part = group_size * seg
        group_ref = group.reshape(1).astype(jnp.int32)
        *packs, low_one = project(
            from_index[0], there_tokens, there_cotangent, vectors[0:2], first, vectors[4:7], own_tables, members, seqs
        )
        backs, tops = [], []
        for i in range(seqs):
            packed = lax.all_to_all(packs[i], ("m", "c"), 0, 0, tiled=True)
            packed = packed.reshape(members, 4, group_size, seg, D // members)
            back, top = attend(flags[i], group_ref, all_tables, packed)
            backs.append(back.reshape(members, 4, part, D // members))
            tops.append(top)
        head = lax.all_to_all(backs[0], ("m", "c"), 0, 0, tiled=True)
        head, tail, later = lax.optimization_barrier((head, backs[1:], later))
        tail = jnp.concatenate(tail, 2)
        tail = lax.all_to_all(tail, ("m", "c"), 0, 0, tiled=True)

        branch, input_part, small_mlp, keep_mlp, send_mlp = mlp(
            from_index[1], to_index[1], tokens.reshape(rows, D), cotangent.reshape(rows, D), vectors[2:4],
            vectors[8:12], vectors[12:13], later,
        )
        tail, keep_mlp = lax.optimization_barrier((tail, keep_mlp))
        input_one, attended, small_rest, keep_attn, send_attn = rest(
            from_index[0], to_index[0], there_tokens, there_cotangent, low_one, vectors[0:2], head, tail, first
        )
        attended = come_home(attended)
        input_one = come_home(input_one)
        weight_out = first[from_index[0][3 * IN_MATRIX :]].reshape(D, D)
        branch_attn = jnp.dot(attended, weight_out, preferred_element_type=F32) + vectors[7]
        mixed = (branch + branch_attn).astype(BF16).reshape(tokens.shape)
        input_grad = (input_part + input_one.astype(F32)).reshape(tokens.shape)

        peaks = jnp.max(jnp.stack(tops)[:, :, :2], (0, 3)).reshape(-1)
        heads_here = HEADS // members
        peak_row = jnp.full((D,), NEG, F32)
        peak_row = lax.dynamic_update_slice(peak_row, peaks, (member * heads_here,))
        small = jnp.concatenate(
            [
                small_rest[3:5], small_mlp[4:6], small_rest[:3], small_mlp[6:7], small_mlp[:4], small_mlp[6:7], peak_row[None],
            ],
            0,
        )
        is_peak = (jnp.arange(14) == 13)[:, None]
        small = butterfly(small, lambda a, b: jnp.where(is_peak, jnp.maximum(a, b), a + b), ("c", "m", "dp", "g"))
        vector_sum, overall_peak = small[:13], small[13, :HEADS]

        def scatter_sum(terms, axes):
            names = ["dp", "g", "m"]
            add = lambda parts: sum(p.astype(F32) for p in parts)
            for axis in axes:
                at = names.index(axis)
                got = []
                for k in range(1, sizes[axis]):
                    to = jnp.bitwise_xor(index[axis], k)
                    sent = add([row_at(t, to, at) for t in terms]).astype(BF16)
                    got.append(swap(sent, axis, k))
                terms = [row_at(t, index[axis], at) for t in terms] + got
                names.remove(axis)
            return add(terms)

        sums = []
        for k, keep, send in ((1, keep_mlp, send_mlp), (0, keep_attn, send_attn)):
            per = pers[k]
            cut = per // 2
            got = swap(send, "c", 1)
            terms = [t.reshape(dp_size, group_size, pair_size, per, BLOCK_ROWS, D) for t in (keep, got)]
            parts = [scatter_sum([t[..., cut:, :, :] for t in terms], ("dp", "m", "g"))]
            if cut:
                parts.insert(0, scatter_sum([t[..., :cut, :, :] for t in terms], ("m", "dp", "g")))
            sums.insert(0, jnp.concatenate(parts, 0))
        sums = jnp.concatenate(sums, 0)

        low_sums = sums.astype(BF16)

        answer, answer_round = local["answer"], local["answer_round"]

        def give_back(turn, own, other):
            got = lax.all_to_all(low_sums[local["backward_index"](turn)], every, 0, 0, tiled=True)
            here = (answer_round == turn)[:, None, None]
            own = jnp.where(here[:capacity], got[answer[:capacity]].astype(F32), own)
            other = jnp.where(here[capacity:], got[answer[capacity:]], other)
            return own, other

        own = sums[local["home_spot"][:capacity]]
        other = low_sums[local["home_spot"][capacity:]]
        own, other = give_back(0, own, other)
        _, own, other = lax.while_loop(
            lambda c: c[0] < plan["rounds"], lambda c: (c[0] + 1,) + give_back(*c), (jnp.int32(1), own, other)
        )
        from_sibling = swap(other, "c", 1).astype(F32)
        owned = jnp.where(local["holds"][:capacity, None, None], own, from_sibling)
        local_block = lax.dynamic_slice_in_dim(plan["slot_block"], me * capacity, capacity)
        holding = (local_block >= 0)[:, None, None]
        owned = jnp.where(holding, owned, 0.0)

        factors = clip_limit / jnp.maximum(overall_peak, clip_limit)
        column_scale = jnp.repeat(jnp.sqrt(factors), HEAD_DIM)
        clipped = ((local_block >= 0) & (local_block // (D // BLOCK_ROWS) < 2))[:, None, None]
        bank_new, first_new, second_new = adamw_update(master, owned, first_moment, second_moment, weight_decay)
        bank_new = jnp.where(clipped, bank_new * column_scale, bank_new)
        bank_new = jnp.where(holding, bank_new, 0.0)
        first_new = jnp.where(holding, first_new, 0.0)
        second_new = jnp.where(holding, second_new, 0.0)
        vector_new, rows_first, rows_second = adamw_update(vectors, vector_sum, vector_first, vector_second, 0.0)
        row_index = jnp.arange(13, dtype=jnp.int32)
        vector_new = jnp.where(
            ((row_index == 4) | (row_index == 5))[:, None], vector_new * column_scale, vector_new
        )
        return (
            mixed, input_grad, owned, bank_new, first_new, second_new, vector_sum, vector_new, rows_first, rows_second, factors,
        )

    return body


def solution(mesh):
    dp_size, ctx_size = mesh.shape["dp"], mesh.shape["ctx"]
    fine = Mesh(
        mesh.devices.reshape(dp_size, GROUPS, ctx_size // GROUPS // 2, 2), ("dp", "g", "m", "c")
    )
    ctx = ("g", "m", "c")
    slots = P(("dp",) + ctx, None, None)
    wide = P("dp", ctx, None)
    in_specs = (wide, P("dp", ctx), wide, slots, slots, slots, P(), P(), P(), P())
    out_specs = (wide, wide, slots, slots, slots, slots, P(), P(), P(), P(), P())
    body = make_body(dict(fine.shape))

    return jax.shard_map(body, mesh=fine, in_specs=in_specs, out_specs=out_specs, check_vma=False)
```
